128 devices in a mesh: tm: 16 (over y, x_lo, core), panel: 8 (over z, x_hi).
Axes of the slice: x: 4 (x_hi: 2, x_lo: 2; x = x_hi * 2 + x_lo), y: 4, z: 4, core: 2. Of those that a mesh axis runs over, the one named last changes fastest.
Arguments:
- forward_element: bfloat16 [3, 16, 1024, 1024], P(None, 'tm', 'panel'), may hold values from -1 to 1
- backward_element: bfloat16 [3, 16, 1024, 1024], P(None, 'tm', 'panel'), may hold values from -1 to 1
Outputs:
- forward_joint: bfloat16 [3, 16, 1024, 1024], P(None, 'tm', 'panel')
- backward_joint: bfloat16 [3, 16, 1024, 1024], P(None, 'tm', 'panel')
The draws below stay inside these ranges and needn't reach their ends.
All inputs are finite; a program needn't handle non-finite values.
Results may differ from the reference program's by a relative error of at most 0.0067.
Values may be sent and summed in bfloat16 or wider, within the bound.
A program may use at most 128 MiB of HBM per device.

```python
import math
import jax
import jax.numpy as jnp
from jax import lax

STATE = 1024
LEVELS = 2
GROUPS = 16


spread_scale = 0.28


def perturbation_field(field_key):
    values = jnp.clip(jax.random.normal(field_key, (GROUPS, STATE, STATE), jnp.float32), -4.0, 4.0)
    return values


def covariance_like(matrix_key):
    subkeys = jax.random.split(matrix_key, 2)
    perturbation = perturbation_field(subkeys[0]) * (spread_scale / math.sqrt(STATE))
    perturbation = (perturbation + jnp.swapaxes(perturbation, 1, 2)) * 0.7071
    diagonal = jnp.exp(jax.random.uniform(subkeys[1], (GROUPS, STATE), jnp.float32, math.log(0.15), math.log(0.5)))
    identity = jnp.eye(STATE, dtype=jnp.float32)
    return perturbation * (1.0 - identity) + identity * diagonal[:, :, None]


def transition_like(matrix_key):
    subkeys = jax.random.split(matrix_key, 2)
    perturbation = perturbation_field(subkeys[0]) * (0.3 / math.sqrt(STATE))
    diagonal = jax.random.uniform(subkeys[1], (GROUPS, STATE), jnp.float32, 0.5, 0.9)
    identity = jnp.eye(STATE, dtype=jnp.float32)
    return perturbation * (1.0 - identity) + identity * diagonal[:, :, None]


def assemble(element_key):
    subkeys = jax.random.split(element_key, 3)
    return jnp.stack([covariance_like(subkeys[0]), transition_like(subkeys[1]), covariance_like(subkeys[2])]).astype(jnp.bfloat16)


def draw_forward_element(key, part):
    return assemble(jax.random.fold_in(key, 101))


def draw_backward_element(key, part):
    return assemble(jax.random.fold_in(key, 202))


def setup_inputs(seed: int = 0) -> dict:
    keys = jax.random.split(jax.random.key(seed), 3)
    return {
        "forward_element": draw_forward_element(jax.random.fold_in(keys[2], 71), 0),
        "backward_element": draw_backward_element(jax.random.fold_in(keys[2], 71), 0),
    }


def matmul(left, right):
    return jnp.dot(left, right, preferred_element_type=jnp.float32)


def combine(partner_cov, partner_trans, partner_info_rows, local_trans, local_info, local_cov_rows, row_start):
    row_count = local_cov_rows.shape[0]
    width = local_trans.shape[0]
    identity = jnp.eye(width, dtype=jnp.float32)
    kernel = matmul(partner_cov, local_info).astype(jnp.bfloat16)
    first_iterate = (identity - kernel).astype(jnp.bfloat16)
    second_iterate = (identity + kernel - matmul(kernel, first_iterate)).astype(jnp.bfloat16)
    local_rows = lax.dynamic_slice_in_dim(local_trans, row_start, row_count, 0)
    factor = matmul(matmul(local_rows, first_iterate).astype(jnp.bfloat16), second_iterate).astype(jnp.bfloat16)
    joint_trans = matmul(factor, partner_trans).astype(jnp.bfloat16)
    middle = matmul(factor, partner_cov).astype(jnp.bfloat16)
    joint_cov = (lax.dot_general(middle, local_trans, (((1,), (1,)), ((), ())), preferred_element_type=jnp.float32) + local_cov_rows).astype(jnp.bfloat16)
    columns = lax.dynamic_slice_in_dim(partner_trans, row_start, row_count, 1)
    upper_rows = lax.dot_general(columns, local_info, (((0,), (0,)), ((), ())), preferred_element_type=jnp.float32).astype(jnp.bfloat16)
    upper_rows = matmul(upper_rows, first_iterate).astype(jnp.bfloat16)
    upper_rows = matmul(upper_rows, second_iterate).astype(jnp.bfloat16)
    joint_info = (matmul(upper_rows, partner_trans) + partner_info_rows).astype(jnp.bfloat16)
    return jnp.stack([joint_cov, joint_trans, joint_info])


def combine_whole(partner, local_element):
    return combine(partner[0], partner[1], partner[2], local_element[1], local_element[2], local_element[0], 0)


def reference(forward_element, backward_element):
    forward = [forward_element[:, position] for position in range(GROUPS)]
    backward = [backward_element[:, position] for position in range(GROUPS)]
    for level_index in range(LEVELS):
        stride = 1 << level_index
        forward = [combine_whole(forward[position - stride], forward[position]) if position >= stride else forward[position] for position in range(GROUPS)]
        backward = [combine_whole(backward[position + stride], backward[position]) if position + stride < GROUPS else backward[position] for position in range(GROUPS)]
    return jnp.stack(forward, axis=1), jnp.stack(backward, axis=1)
```

```python
import jax
import jax.numpy as jnp
from jax import lax
from jax.experimental import pallas as pl
from jax.experimental.pallas import tpu as pltpu
from jax.sharding import PartitionSpec as P

MESH = pl.DeviceIdType.MESH
C, A, J = 0, 1, 2
BF = jnp.bfloat16
F32 = jnp.float32


def kernel(fwd, bwd, out, own, away, gat1, gat2, kmat, work, cov1, res, add1, add2, lsem, xs, xr, cs, cr,
           qs, ps, zr, rs, vs, vr, las, ads, adr, c2s, c2r, p2s, p2r, v2s, v2r, outs, outr):
    n = gat1.shape[-1]
    rows = n // 4
    half = rows // 2
    tm = lax.axis_index("tm")
    p = lax.axis_index("panel")
    c = lax.rem(tm, 2)
    k = lax.div(tm, 2)
    z = lax.div(p, 2)
    d = lax.rem(p, 2)
    q = lax.div(z, 2)
    sgn = 1 - 2 * d
    same = c == q
    cross = c != d
    zc = 3 - z
    zp = z + 1 - 2 * lax.rem(z, 2)
    r = jnp.where(same, z, zc)
    tau = jnp.where(same, 0, 1)
    psl = jnp.where(cross, 1, 0)
    segment = 2 * k + q
    partner = (tm, 2 * zp + d)
    sibling = (tm + 1 - 2 * c, p)
    twin = (tm, 2 * z + 1 - d)
    following = (lax.rem(tm + 2 * sgn + 16, 16), p)

    def copy(src, dst, ssem, rsem, dev):
        return pltpu.make_async_remote_copy(src, dst, ssem, rsem, device_id=dev, device_id_type=MESH)

    def block(i):
        return pl.ds(pl.multiple_of(i * rows, rows), rows)

    pending = []

    def send(src, dst, ssem, rsem, dev):
        cp = copy(src, dst, ssem, rsem, dev)
        cp.start()
        return cp

    def arrived(dst, ssem, rsem):
        copy(dst, dst, ssem, rsem, partner).wait_recv()

    mine = pl.ds(pl.multiple_of(d * half, half), half)
    theirs = pl.ds(pl.multiple_of((1 - d) * half, half), half)

    def load(src_own, src_away):
        pltpu.make_async_copy(src_own, own.at[0, :, mine], lsem.at[0]).start()
        pltpu.make_async_copy(src_away, away, lsem.at[1]).start()

    @pl.when(d == 0)
    def _():
        load(fwd, bwd)

    @pl.when(d == 1)
    def _():
        load(bwd, fwd)

    pltpu.make_async_copy(away, away, lsem.at[1]).wait()
    for m in (J, C, A):
        pending.append(send(away.at[m], own.at[0, m, mine], xs.at[m], xr.at[m], twin))
    pltpu.make_async_copy(own.at[0, :, mine], own.at[0, :, mine], lsem.at[0]).wait()

    def xwait(m):
        arrived(own.at[0, m, theirs], xs.at[m], xr.at[m])

    def crossing(m):
        return copy(own.at[0, m], own.at[1, m], cs.at[m], cr.at[m], following)

    kind_q = jnp.where(same, 0, 1)
    kind_p = 1 - kind_q
    to_q = (tm, 2 * jnp.where(same, zp, zc) + d)
    to_p = (tm, 2 * jnp.where(same, zc, zp) + d)

    def qcopy(j, m):
        return copy(own.at[0, m], gat1.at[0, j, block(z)], qs.at[j], zr.at[kind_q, j], to_q)

    def pcopy(j, m):
        return copy(own.at[psl, m], gat1.at[1, j, block(z)], ps.at[j], zr.at[kind_p, j], to_p)

    own_slot = jnp.where(same, 0, psl)

    def owncopy(j):
        m = jnp.where(same, J, C) if j == 0 else A
        local = pltpu.make_async_copy(own.at[own_slot, m], gat1.at[tau, j, block(z)], las.at[j])
        side = copy(own.at[own_slot, m], gat1.at[tau, j, block(z)], vs.at[3, j], vr.at[3, j], sibling)
        return local, side

    def start_own(j):
        for cp in owncopy(j):
            cp.start()

    xwait(J)
    qcopy(0, J).start()
    xwait(C)

    @pl.when(cross)
    def _():
        crossing(C).start()

    @pl.when(jnp.logical_not(cross))
    def _():
        pcopy(0, C).start()

    xwait(A)

    @pl.when(cross)
    def _():
        crossing(A).start()
        crossing(J).start()

    qcopy(1, A).start()

    @pl.when(cross)
    def _():
        crossing(C).wait_recv()
        pcopy(0, C).start()
        crossing(A).wait_recv()

    start_own(0)
    pcopy(1, A).start()
    start_own(1)

    @pl.when(cross)
    def _():
        crossing(J).wait_recv()

    aux_there = (2 * k + q, 2 * zc + d)
    which = jnp.where(same, 1, 0)

    def addend():
        return copy(own.at[jnp.where(same, psl, 0), jnp.where(same, J, C)], add1.at[which], ads.at[0],
                    adr.at[which], aux_there)

    def addend_side():
        return copy(own.at[psl, J], add1.at[1], ads.at[1], adr.at[1], sibling)

    def addend_local():
        return pltpu.make_async_copy(own.at[0, C], add1.at[0], adr.at[0])

    addend().start()

    @pl.when(jnp.logical_not(same))
    def _():
        addend_side().start()

    @pl.when(same)
    def _():
        addend_local().start()

    last = 3 - zp

    def relay(j):
        return copy(gat1.at[tau, j, block(zc)], gat1.at[tau, j, block(zc)], rs.at[j], zr.at[2, j], partner)

    def side(kind, j, b):
        return copy(gat1.at[tau, j, block(b)], gat1.at[tau, j, block(b)], vs.at[kind, j], vr.at[kind, j], sibling)

    def take(kind, j, b):
        arrived(gat1.at[tau, j, block(b)], rs.at[j], zr.at[kind, j])
        if kind == 1:
            relay(j).start()
        side(kind, j, b).start()

    def side_arrived(j, kinds):
        for kind, b in ((3, z), (1, zc), (0, zp), (2, last)):
            if kind in kinds:
                arrived(gat1.at[1 - tau, j, block(b)], vs.at[kind, j], vr.at[kind, j])

    take(1, 0, zc)
    take(0, 0, zp)
    take(1, 1, zc)
    take(0, 1, zp)
    take(2, 0, last)
    for j in range(2):
        owncopy(j)[0].wait()
    side_arrived(0, (0, 1, 2, 3))
    side_arrived(1, (1,))

    def dot(a, b):
        return jnp.dot(a, b, preferred_element_type=F32)

    tiles = [slice(i * rows, (i + 1) * rows) for i in range(4)]

    def fill_k(gat):
        @pl.loop(0, 4)
        def _(b):
            for t in tiles:
                kmat[block(b), t] = dot(gat[1, 0, block(b), :], gat[0, 0, :, t]).astype(BF)

    def chain(src, tmp, dst):
        for t in tiles:
            work[3, :, t] = (work[src, :, t].astype(F32) - dot(work[src], kmat[:, t])).astype(BF)
        for t in tiles:
            work[tmp, :, t] = dot(work[3], kmat[:, t]).astype(BF)
        for t in tiles:
            work[dst, :, t] = (work[3, :, t].astype(F32) + dot(work[tmp], kmat[:, t])).astype(BF)

    def early(gat):
        fill_k(gat)
        work[0] = gat[0, 1, block(r), :]
        chain(0, 1, 0)
        for t in tiles:
            work[2, :, t] = dot(work[0], gat[1, 0, :, t]).astype(BF)

    def cov(gat, t, base):
        prod = lax.dot_general(work[2], gat[0, 1, t, :], (((1,), (1,)), ((), ())), preferred_element_type=F32)
        return (prod + base.astype(F32)).astype(BF)

    def info(gat):
        columns = gat[1, 1, :, block(r)]
        for t in tiles:
            work[1, :, t] = lax.dot_general(columns, gat[0, 0, :, t], (((0,), (0,)), ((), ())),
                                            preferred_element_type=F32).astype(BF)
        chain(1, 2, 1)

    early(gat1)
    take(2, 1, last)
    side_arrived(1, (0, 2, 3))

    first = jnp.where(d == 0, segment >= 1, segment < 15)
    second = jnp.where(d == 0, segment >= 2, segment < 14)

    arrived(add1.at[0], ads.at[0], adr.at[0])
    for t in tiles:
        base = add1[0, :, t]
        cov1[:, t] = jnp.where(first, cov(gat1, t, base), base)

    def cross2(j):
        if j == 0:
            return copy(cov1, gat2.at[1, 0, block(r)], c2s.at[0], c2r.at[0], following)
        if j == 1:
            return copy(gat2.at[0, 1, block(r)], gat2.at[1, 1, block(r)], c2s.at[1], c2r.at[1], following)
        return copy(gat2.at[0, 0, block(r)], add2, c2s.at[2], c2r.at[2], following)

    def pair2(kind, j):
        ref = gat2.at[kind, j, block(r)]
        return copy(ref, ref, p2s.at[kind, j], p2r.at[kind, j], partner)

    rp = jnp.where(same, zp, last)

    def side2(hop, kind, j):
        ref = gat2.at[kind, j, block(rp if hop else r)]
        return copy(ref, ref, v2s.at[hop, kind, j], v2r.at[hop, kind, j], sibling)

    cross2(0).start()
    for t in tiles:
        gat2[0, 1, block(r), t] = jnp.where(first, dot(work[0], gat1[1, 1, :, t]).astype(BF),
                                            gat1[0, 1, block(r), t])
    cross2(1).start()
    pair2(0, 1).start()
    side2(0, 0, 1).start()

    info(gat1)
    arrived(add1.at[1], ads.at[0], adr.at[1])
    for t in tiles:
        value = (dot(work[1], gat1[1, 1, :, t]) + add1[1, :, t].astype(F32)).astype(BF)
        gat2[0, 0, block(r), t] = jnp.where(first, value, gat1[0, 0, block(r), t])
    pair2(0, 0).start()
    side2(0, 0, 0).start()

    def p_arrived(j):
        arrived(gat2.at[1, j, block(r)], c2s.at[j], c2r.at[j])
        pair2(1, j).start()
        side2(0, 1, j).start()

    def pair_arrived(kind, j):
        arrived(gat2.at[kind, j, block(rp)], p2s.at[kind, j], p2r.at[kind, j])
        side2(1, kind, j).start()

    rq = jnp.where(same, zc, z)
    rpq = jnp.where(same, last, zp)

    def side2_arrived(kind, j):
        arrived(gat2.at[kind, j, block(rq)], v2s.at[0, kind, j], v2r.at[0, kind, j])
        arrived(gat2.at[kind, j, block(rpq)], v2s.at[1, kind, j], v2r.at[1, kind, j])

    p_arrived(0)
    cross2(2).start()
    p_arrived(1)
    pair_arrived(0, 1)
    pair_arrived(0, 0)
    pair_arrived(1, 0)
    side2_arrived(0, 0)
    side2_arrived(1, 0)
    early(gat2)
    side2_arrived(0, 1)

    target = 2 * k + q

    def deliver(m, hf):
        return copy(res.at[m, pl.ds(hf * half, half)], out.at[d, m], outs.at[hf, m], outr.at[d, m],
                    (target, 2 * r + hf))

    def deliver_own(m, hf):
        return pltpu.make_async_copy(res.at[m, pl.ds(hf * half, half)], out.at[d, m], outs.at[hf, m])

    def deliver_all(m, act):
        for hf in range(2):
            stays = jnp.logical_and(same, d == hf)

            @pl.when(stays)
            def _():
                act(deliver_own(m, hf), False)

            @pl.when(jnp.logical_not(stays))
            def _():
                act(deliver(m, hf), True)

    def begin(cp, remote):
        cp.start()

    def finish(cp, remote):
        if remote:
            cp.wait_send()
        else:
            cp.wait()

    for t in tiles:
        base = cov1[:, t]
        res[C, :, t] = jnp.where(second, cov(gat2, t, base), base)
    deliver_all(C, begin)
    pair_arrived(1, 1)
    side2_arrived(1, 1)
    for t in tiles:
        res[A, :, t] = jnp.where(second, dot(work[0], gat2[1, 1, :, t]).astype(BF), gat2[0, 1, block(r), t])
    deliver_all(A, begin)
    info(gat2)
    arrived(add2, c2s.at[2], c2r.at[2])
    for t in tiles:
        value = (dot(work[1], gat2[1, 1, :, t]) + add2[:, t].astype(F32)).astype(BF)
        res[J, :, t] = jnp.where(second, value, gat2[0, 0, block(r), t])
    deliver_all(J, begin)

    for cp in pending:
        cp.wait_send()
    for j, m in ((0, J), (1, A)):
        qcopy(j, m).wait_send()
    for j, m in ((0, C), (1, A)):
        pcopy(j, m).wait_send()

    @pl.when(cross)
    def _():
        for m in (C, A, J):
            crossing(m).wait_send()

    addend().wait_send()

    @pl.when(jnp.logical_not(same))
    def _():
        addend_side().wait_send()

    for j in range(2):
        owncopy(j)[1].wait_send()
        relay(j).wait_send()
        for kind, b in ((1, zc), (0, zp), (2, last)):
            side(kind, j, b).wait_send()
    for j in range(3):
        cross2(j).wait_send()
    for kind in range(2):
        for j in range(2):
            pair2(kind, j).wait_send()
            for hop in range(2):
                side2(hop, kind, j).wait_send()
    for m in range(3):
        deliver_all(m, finish)
    for m in range(3):
        arrived(out.at[1 - d, m], outs.at[0, m], outr.at[1 - d, m])

        @pl.when(jnp.logical_not(same))
        def _():
            arrived(out.at[d, m], outs.at[0, m], outr.at[d, m])


def shards(forward_element, backward_element):
    fwd = forward_element[:, 0]
    bwd = backward_element[:, 0]
    _, half, n = fwd.shape
    rows = n // 4
    dma = pltpu.SemaphoreType.DMA
    anywhere = pl.BlockSpec(memory_space=pl.ANY)
    joint = pl.pallas_call(
        kernel,
        out_shape=jax.ShapeDtypeStruct((2, 3, half, n), BF),
        in_specs=[anywhere, anywhere],
        out_specs=anywhere,
        scratch_shapes=[
            pltpu.VMEM((2, 3, rows, n), BF),
            pltpu.VMEM((3, half, n), BF),
            pltpu.VMEM((2, 2, n, n), BF),
            pltpu.VMEM((2, 2, n, n), BF),
            pltpu.VMEM((n, n), BF),
            pltpu.VMEM((4, rows, n), BF),
            pltpu.VMEM((rows, n), BF),
            pltpu.VMEM((3, rows, n), BF),
            pltpu.VMEM((2, rows, n), BF),
            pltpu.VMEM((rows, n), BF),
            dma((2,)), dma((3,)), dma((3,)), dma((3,)), dma((3,)),
            dma((2,)), dma((2,)), dma((3, 2)), dma((2,)), dma((4, 2)), dma((4, 2)), dma((2,)), dma((2,)), dma((2,)),
            dma((3,)), dma((3,)), dma((2, 2)), dma((2, 2)), dma((2, 2, 2)), dma((2, 2, 2)), dma((2, 3)), dma((2, 3)),
        ],
        compiler_params=pltpu.CompilerParams(has_side_effects=True, vmem_limit_bytes=60000 * 1024),
    )(fwd, bwd)
    return (joint[0][:, None], joint[1][:, None])


def solution(mesh):
    spec = P(None, "tm", "panel", None)
    return jax.shard_map(shards, mesh=mesh, in_specs=(spec, spec), out_specs=(spec, spec), check_vma=False)
```

```python
import jax
import jax.numpy as jnp
from jax import lax
from jax.experimental import pallas as pl
from jax.experimental.pallas import tpu as pltpu
from jax.sharding import PartitionSpec as P

MESH = pl.DeviceIdType.MESH
C, A, J = 0, 1, 2
JQ, CP, AQ, AP = 0, 1, 2, 3
BF = jnp.bfloat16
F32 = jnp.float32


def kernel(fwd, bwd, out, st, gat1, gat2, kmat, wa, wt, wl, wg, cov1, res, addc, addj, add2,
           xs, xr, zs, zr, rs, vs, vr, las, acs, acr, ajs, ajr, afs, afr,
           c2s, c2r, p2s, p2r, v2s, v2r, outs, outr):
    n = gat1.shape[-1]
    rows = n // 4
    half = rows // 2
    wide = n // 2
    tm = lax.axis_index("tm")
    p = lax.axis_index("panel")
    c = lax.rem(tm, 2)
    k = lax.div(tm, 2)
    z = lax.div(p, 2)
    d = lax.rem(p, 2)
    q = lax.div(z, 2)
    sgn = 1 - 2 * d
    same = c == q
    aux = jnp.logical_not(same)
    zc = 3 - z
    zp = z + 1 - 2 * lax.rem(z, 2)
    last = 3 - zp
    r = jnp.where(same, z, zc)
    rp = jnp.where(same, zp, last)
    rq = jnp.where(same, zc, z)
    rpq = jnp.where(same, last, zp)
    segment = 2 * k + q
    flip = tm + 1 - 2 * c
    partner = (tm, 2 * zp + d)
    across = (tm, 2 * zc + d)
    sibling = (flip, p)
    following = (lax.rem(tm + 2 * sgn + 16, 16), p)
    preceding = (lax.rem(tm - 2 * sgn + 16, 16), p)

    def copy(src, dst, ssem, rsem, dev):
        return pltpu.make_async_remote_copy(src, dst, ssem, rsem, device_id=dev, device_id_type=MESH)

    def block(i):
        return pl.ds(pl.multiple_of(i * rows, rows), rows)

    def piece(i, hh):
        return pl.ds(pl.multiple_of(i * rows + hh * half, half), half)

    def arrived(dst, ssem, rsem):
        copy(dst, dst, ssem, rsem, partner).wait_recv()

    barrier = pltpu.get_barrier_semaphore()

    def greet(dev):
        pl.semaphore_signal(barrier, inc=1, device_id=dev, device_id_type=MESH)

    before = lax.rem(k - sgn + 8, 8)
    greet(sibling)
    for core in range(2):
        greet((2 * k + core, 2 * z + 1 - d))
        greet((2 * before + 1 - d, 2 * z + core))
    greet(partner)
    greet(across)
    greet(preceding)

    @pl.when(aux)
    def _():
        for hh in range(2):
            greet((flip, 2 * zc + hh))

    pl.semaphore_wait(barrier, jnp.where(aux, 10, 8))

    ins = (fwd, bwd)
    mats = (J, C, A, A)

    def column(dd):
        return lax.rem(k + jnp.where(c == dd, 0, 1 - 2 * dd) + 8, 8)

    def scatter(m, dd, hf):
        src = ins[dd].at[mats[m], :, pl.ds(hf * wide, wide)]
        slot = c if m in (JQ, AQ) else 1 - c
        col = k if m in (JQ, AQ) else column(dd)
        dst = st.at[slot, m, pl.ds(pl.multiple_of(d * half, half), half)]
        remote = copy(src, dst, xs.at[m, dd, hf], xr.at[slot, m, d], (2 * col + hf, 2 * z + dd))
        local = pltpu.make_async_copy(src, dst, xr.at[slot, m, d])
        stays = jnp.logical_and(d == dd, c == hf)
        if m == CP:
            stays = jnp.logical_and(stays, c == dd)
        return local, remote, stays

    def scatter_all(m, act_local, act_remote):
        for dd in range(2):
            for hf in range(2):
                local, remote, stays = scatter(m, dd, hf)
                if m == AP:

                    @pl.when(c != dd)
                    def _():
                        act_remote(remote)

                else:

                    @pl.when(stays)
                    def _():
                        act_local(local)

                    @pl.when(jnp.logical_not(stays))
                    def _():
                        act_remote(remote)

    def begin(cp):
        cp.start()

    def sent(cp):
        cp.wait_send()

    def nothing(cp):
        pass

    def addend_c(dd, act_local, act_remote):
        src = ins[dd].at[C]
        dst = addc.at[pl.ds(pl.multiple_of(d * half, half), half)]
        to = (jnp.where(same, tm, flip), jnp.where(same, 2 * z + dd, 2 * zc + dd))
        remote = copy(src, dst, acs.at[dd], acr.at[d], to)
        stays = jnp.logical_and(same, d == dd)

        @pl.when(stays)
        def _():
            act_local(pltpu.make_async_copy(src, dst, acr.at[d]))

        @pl.when(jnp.logical_not(stays))
        def _():
            act_remote(remote)

    def addend_j(dd):
        dst = addj.at[0, pl.ds(pl.multiple_of(d * half, half), half)]
        return copy(ins[dd].at[J], dst, ajs.at[dd], ajr.at[d], (2 * column(dd) + 1 - c, 2 * z + dd))

    for m in (JQ, CP, AQ, AP):
        scatter_all(m, begin, begin)
    for dd in range(2):
        addend_c(dd, begin, begin)
        addend_j(dd).start()

    mycols = pl.ds(pl.multiple_of(c * wide, wide), wide)
    sibcols = pl.ds(pl.multiple_of((1 - c) * wide, wide), wide)

    def staged(pair, m):
        if m == AP:
            return st.at[d, jnp.where(pair == d, AP, AQ)]
        return st.at[pair, m]

    def hrows(hh):
        return pl.ds(pl.multiple_of(hh * half, half), half)

    def zcopy(pair, m, hh):
        kind = jnp.where(pair == q, 0, 1)
        to = (tm, 2 * jnp.where(pair == q, zp, zc) + d)
        return copy(staged(pair, m).at[hrows(hh)], gat1.at[m, piece(z, hh), mycols], zs.at[pair, m, hh],
                    zr.at[kind, m, hh], to)

    def zsend(pair, m, hh, fresh=True):
        if fresh:
            arrived(st.at[pair, m, hrows(hh)], xs.at[m, 0, 0], xr.at[pair, m, hh])
        zcopy(pair, m, hh).start()

    def owncopy(m):
        src = staged(q, m)
        dst = gat1.at[m, block(z), mycols]
        return pltpu.make_async_copy(src, dst, las.at[m]), copy(src, dst, vs.at[3, m], vr.at[3, m], sibling)

    def start_own(m):
        for cp in owncopy(m):
            cp.start()

    def relay(m, hh):
        ref = gat1.at[m, piece(zc, hh), mycols]
        return copy(ref, ref, rs.at[m, hh], zr.at[2, m, hh], partner)

    def side(kind, m, b):
        ref = gat1.at[m, block(b), mycols]
        return copy(ref, ref, vs.at[kind, m], vr.at[kind, m], sibling)

    source = {0: zp, 1: zc, 2: last}

    def take(kind, m):
        for hh in range(2):
            arrived(gat1.at[m, piece(source[kind], hh), mycols], rs.at[m, hh], zr.at[kind, m, hh])
            if kind == 1:
                relay(m, hh).start()
        side(kind, m, source[kind]).start()

    def side_arrived(m):
        owncopy(m)[0].wait()
        for kind, b in ((3, z), (1, zc), (0, zp), (2, last)):
            arrived(gat1.at[m, block(b), sibcols], vs.at[kind, m], vr.at[kind, m])

    zsend(q, JQ, d)
    zsend(1 - q, JQ, d)
    zsend(1 - d, CP, d)
    zsend(q, AQ, d)
    zsend(1 - q, AQ, d)
    zsend(q, JQ, 1 - d)
    zsend(1 - q, JQ, 1 - d)
    start_own(JQ)
    zsend(d, CP, d)
    zsend(1 - d, CP, 1 - d)
    zsend(d, CP, 1 - d)
    start_own(CP)
    zsend(q, AQ, 1 - d)
    zsend(1 - q, AQ, 1 - d)
    start_own(AQ)
    take(1, JQ)
    zsend(1 - d, AP, d, False)
    zsend(1 - d, AP, 1 - d, False)
    zsend(d, AP, d)
    zsend(d, AP, 1 - d)
    start_own(AP)
    take(1, CP)
    take(1, AQ)
    take(0, JQ)
    take(0, CP)
    take(1, AP)
    take(0, AQ)
    take(0, AP)

    for hh in range(2):
        arrived(addj.at[0, hrows(hh)], ajs.at[0], ajr.at[hh])

    def addend_on():
        return copy(addj.at[0], addj.at[1], afs.at[0], afr.at[0], (flip, 2 * zc + d))

    @pl.when(aux)
    def _():
        addend_on().start()

    take(2, JQ)
    take(2, CP)

    def dot(a, b):
        return jnp.dot(a, b, preferred_element_type=F32)

    tiles = [slice(i * rows, (i + 1) * rows) for i in range(4)]

    def fill_k(gat):
        @pl.loop(0, 4)
        def _(b):
            for t in tiles:
                kmat[block(b), t] = dot(gat[CP, block(b), :], gat[JQ, :, t]).astype(BF)

    def chain(count):
        s = slice(0, count)
        for t in tiles:
            wl[s, t] = (wa[s, t].astype(F32) - dot(wa[s, :], kmat[:, t])).astype(BF)
        for t in tiles:
            wt[s, t] = dot(wl[s, :], kmat[:, t]).astype(BF)
        for t in tiles:
            wa[s, t] = (wl[s, t].astype(F32) + dot(wt[s, :], kmat[:, t])).astype(BF)

    top = slice(0, rows)
    low = slice(rows, 2 * rows)

    def middle(gat):
        for t in tiles:
            wg[:, t] = dot(wa[top, :], gat[CP, :, t]).astype(BF)

    def cov(gat, t, base):
        prod = lax.dot_general(wg[...], gat[AQ, t, :], (((1,), (1,)), ((), ())), preferred_element_type=F32)
        return (prod + base.astype(F32)).astype(BF)

    def info(gat):
        columns = gat[AP, :, block(r)]
        for t in tiles:
            wa[top, t] = lax.dot_general(columns, gat[JQ, :, t], (((0,), (0,)), ((), ())),
                                         preferred_element_type=F32).astype(BF)
        chain(rows)

    side_arrived(JQ)
    side_arrived(CP)
    fill_k(gat1)
    take(2, AQ)
    side_arrived(AQ)
    wa[top, :] = gat1[AQ, block(r), :]
    wa[low, :] = gat1[AQ, block(rp), :]
    chain(2 * rows)
    middle(gat1)

    first = jnp.where(d == 0, segment >= 1, segment < 15)
    second = jnp.where(d == 0, segment >= 2, segment < 14)

    for hh in range(2):
        arrived(addc.at[hrows(hh)], acs.at[0], acr.at[hh])
    for t in tiles:
        base = addc[:, t]
        cov1[:, t] = jnp.where(first, cov(gat1, t, base), base)

    left = slice(0, wide)
    right = slice(wide, n)

    def cross2(i):
        src, dst = (
            (cov1, gat2.at[CP, block(r)]),
            (gat2.at[AQ, block(r)], gat2.at[AP, block(r)]),
            (gat2.at[AQ, block(rp), left], gat2.at[AP, block(rp), left]),
            (gat2.at[JQ, block(r)], add2),
        )[i]
        return copy(src, dst, c2s.at[i], c2r.at[i], following)

    pair_refs = (
        lambda b: gat2.at[JQ, block(b)],
        lambda b: gat2.at[CP, block(b)],
        lambda b: gat2.at[AP, block(b), right],
    )

    def pair2(i):
        ref = pair_refs[i](r)
        return copy(ref, ref, p2s.at[i], p2r.at[i], partner)

    def pair_wait(i):
        arrived(pair_refs[i](rp), p2s.at[i], p2r.at[i])

    side_refs = (
        lambda a, b: gat2.at[JQ, block(a)],
        lambda a, b: gat2.at[JQ, block(b)],
        lambda a, b: gat2.at[CP, block(a)],
        lambda a, b: gat2.at[CP, block(b)],
        lambda a, b: gat2.at[AQ, block(a)],
        lambda a, b: gat2.at[AQ, block(b)],
        lambda a, b: gat2.at[AP, block(a)],
        lambda a, b: gat2.at[AP, block(b), left],
        lambda a, b: gat2.at[AP, block(b), right],
    )

    def side2(i):
        ref = side_refs[i](r, rp)
        return copy(ref, ref, v2s.at[i], v2r.at[i], sibling)

    def side2_wait(*which):
        for i in which:
            arrived(side_refs[i](rq, rpq), v2s.at[i], v2r.at[i])

    cross2(0).start()
    take(2, AP)
    side_arrived(AP)
    for s, b in ((top, r), (low, rp)):
        edge = first
        for t in tiles:
            gat2[AQ, block(b), t] = jnp.where(edge, dot(wa[s, :], gat1[AP, :, t]).astype(BF),
                                              gat1[AQ, block(b), t])
    cross2(1).start()
    cross2(2).start()
    side2(4).start()
    side2(5).start()
    arrived(gat2.at[CP, block(r)], c2s.at[0], c2r.at[0])
    pair2(1).start()
    side2(2).start()

    info(gat1)
    mine = jnp.where(same, 0, 1)

    @pl.when(aux)
    def _():
        arrived(addj.at[1], afs.at[0], afr.at[0])

    for t in tiles:
        value = (dot(wa[top, :], gat1[AP, :, t]) + addj[mine, :, t].astype(F32)).astype(BF)
        gat2[JQ, block(r), t] = jnp.where(first, value, gat1[JQ, block(r), t])
    pair2(0).start()
    side2(0).start()
    cross2(3).start()

    arrived(gat2.at[AP, block(r)], c2s.at[1], c2r.at[1])
    pair2(2).start()
    side2(6).start()
    pair_wait(1)
    side2(3).start()
    pair_wait(0)
    side2(1).start()
    side2_wait(0, 1, 2, 3)
    fill_k(gat2)
    wa[top, :] = gat2[AQ, block(r), :]
    chain(rows)
    middle(gat2)

    target = 2 * k + q

    def deliver_all(m, act_local, act_remote):
        for hf in range(2):
            stays = jnp.logical_and(same, d == hf)
            src = res.at[m, pl.ds(hf * half, half)]

            @pl.when(stays)
            def _():
                act_local(pltpu.make_async_copy(src, out.at[d, m], outs.at[hf, m]))

            @pl.when(jnp.logical_not(stays))
            def _():
                act_remote(copy(src, out.at[d, m], outs.at[hf, m], outr.at[d, m], (target, 2 * r + hf)))

    def done(cp):
        cp.wait()

    side2_wait(4, 5)
    for t in tiles:
        base = cov1[:, t]
        res[C, :, t] = jnp.where(second, cov(gat2, t, base), base)
    deliver_all(C, begin, begin)

    arrived(gat2.at[AP, block(rp), left], c2s.at[2], c2r.at[2])
    side2(7).start()
    pair_wait(2)
    side2(8).start()
    side2_wait(6, 7, 8)
    for t in tiles:
        res[A, :, t] = jnp.where(second, dot(wa[top, :], gat2[AP, :, t]).astype(BF), gat2[AQ, block(r), t])
    deliver_all(A, begin, begin)
    info(gat2)
    arrived(add2, c2s.at[3], c2r.at[3])
    for t in tiles:
        value = (dot(wa[top, :], gat2[AP, :, t]) + add2[:, t].astype(F32)).astype(BF)
        res[J, :, t] = jnp.where(second, value, gat2[JQ, block(r), t])
    deliver_all(J, begin, begin)

    for m in (JQ, CP, AQ, AP):
        scatter_all(m, nothing, sent)
        owncopy(m)[1].wait_send()
        for hh in range(2):
            relay(m, hh).wait_send()
            for pair in range(2):
                zcopy(pair, m, hh).wait_send()
        for kind in range(3):
            side(kind, m, source[kind]).wait_send()
    for dd in range(2):
        addend_c(dd, nothing, sent)
        addend_j(dd).wait_send()

    @pl.when(aux)
    def _():
        addend_on().wait_send()

    for i in range(4):
        cross2(i).wait_send()
    for i in range(3):
        pair2(i).wait_send()
    for i in range(9):
        side2(i).wait_send()
    for m in range(3):
        deliver_all(m, done, sent)
    for m in range(3):
        arrived(out.at[1 - d, m], outs.at[0, m], outr.at[1 - d, m])

        @pl.when(aux)
        def _():
            arrived(out.at[d, m], outs.at[0, m], outr.at[d, m])


def shards(forward_element, backward_element):
    fwd = forward_element[:, 0]
    bwd = backward_element[:, 0]
    _, half, n = fwd.shape
    rows = n // 4
    dma = pltpu.SemaphoreType.DMA
    anywhere = pl.BlockSpec(memory_space=pl.ANY)
    joint = pl.pallas_call(
        kernel,
        out_shape=jax.ShapeDtypeStruct((2, 3, half, n), BF),
        in_specs=[anywhere, anywhere],
        out_specs=anywhere,
        scratch_shapes=[
            pltpu.VMEM((2, 4, rows, n // 2), BF),
            pltpu.VMEM((4, n, n), BF),
            pltpu.VMEM((4, n, n), BF),
            pltpu.VMEM((n, n), BF),
            pltpu.VMEM((2 * rows, n), BF),
            pltpu.VMEM((2 * rows, n), BF),
            pltpu.VMEM((2 * rows, n), BF),
            pltpu.VMEM((rows, n), BF),
            pltpu.VMEM((rows, n), BF),
            pltpu.VMEM((3, rows, n), BF),
            pltpu.VMEM((rows, n), BF),
            pltpu.VMEM((2, rows, n), BF),
            pltpu.VMEM((rows, n), BF),
            dma((4, 2, 2)), dma((2, 4, 2)), dma((2, 4, 2)), dma((3, 4, 2)), dma((4, 2)), dma((4, 4)), dma((4, 4)),
            dma((4,)), dma((2,)), dma((2,)), dma((2,)), dma((2,)), dma((1,)), dma((1,)),
            dma((4,)), dma((4,)), dma((3,)), dma((3,)), dma((9,)), dma((9,)), dma((2, 3)), dma((2, 3)),
        ],
        compiler_params=pltpu.CompilerParams(
            has_side_effects=True, collective_id=0, vmem_limit_bytes=60000 * 1024
        ),
    )(fwd, bwd)
    return (joint[0][:, None], joint[1][:, None])


def solution(mesh):
    spec = P(None, "tm", "panel", None)
    return jax.shard_map(shards, mesh=mesh, in_specs=(spec, spec), out_specs=(spec, spec), check_vma=False)
```

```python
import jax
import jax.numpy as jnp
from jax import lax
from jax.experimental import pallas as pl
from jax.experimental.pallas import tpu as pltpu
from jax.sharding import PartitionSpec as P

MESH = pl.DeviceIdType.MESH
C, A, J = 0, 1, 2
JQ, CP, AQ, AP = 0, 1, 2, 3
BF = jnp.bfloat16
F32 = jnp.float32


def kernel(fwd, bwd, out, st, gat1, gat2, kmat, wa, wt, wl, wg, cov1, res, addc, addj, add2,
           xs, xr, zs, zr, rs, vs, vr, las, acs, acr, ajs, ajr, afs, afr,
           c2s, c2r, p2s, p2r, v2s, v2r, outs, outr):
    n = gat1.shape[-1]
    rows = n // 4
    half = rows // 2
    wide = n // 2
    tm = lax.axis_index("tm")
    p = lax.axis_index("panel")
    c = lax.rem(tm, 2)
    k = lax.div(tm, 2)
    z = lax.div(p, 2)
    d = lax.rem(p, 2)
    q = lax.div(z, 2)
    sgn = 1 - 2 * d
    same = c == q
    aux = jnp.logical_not(same)
    zc = 3 - z
    zp = z + 1 - 2 * lax.rem(z, 2)
    last = 3 - zp
    r = jnp.where(same, z, zc)
    rp = jnp.where(same, zp, last)
    rq = jnp.where(same, zc, z)
    rpq = jnp.where(same, last, zp)
    segment = 2 * k + q
    flip = tm + 1 - 2 * c
    partner = (tm, 2 * zp + d)
    across = (tm, 2 * zc + d)
    sibling = (flip, p)
    following = (lax.rem(tm + 2 * sgn + 16, 16), p)
    preceding = (lax.rem(tm - 2 * sgn + 16, 16), p)

    def copy(src, dst, ssem, rsem, dev):
        return pltpu.make_async_remote_copy(src, dst, ssem, rsem, device_id=dev, device_id_type=MESH)

    def block(i):
        return pl.ds(pl.multiple_of(i * rows, rows), rows)

    def piece(i, hh):
        return pl.ds(pl.multiple_of(i * rows + hh * half, half), half)

    def arrived(dst, ssem, rsem):
        copy(dst, dst, ssem, rsem, partner).wait_recv()

    barrier = pltpu.get_barrier_semaphore()

    def greet(dev):
        pl.semaphore_signal(barrier, inc=1, device_id=dev, device_id_type=MESH)

    before = lax.rem(k - sgn + 8, 8)
    greet(sibling)
    for core in range(2):
        greet((2 * k + core, 2 * z + 1 - d))
        greet((2 * before + 1 - d, 2 * z + core))
    greet(partner)
    greet(across)
    greet(preceding)

    @pl.when(aux)
    def _():
        for hh in range(2):
            greet((flip, 2 * zc + hh))

    pl.semaphore_wait(barrier, jnp.where(aux, 10, 8))

    ins = (fwd, bwd)
    mats = (J, C, A, A)

    def column(dd):
        return lax.rem(k + jnp.where(c == dd, 0, 1 - 2 * dd) + 8, 8)

    def scatter(m, dd, hf):
        src = ins[dd].at[mats[m], :, pl.ds(hf * wide, wide)]
        slot = c if m in (JQ, AQ) else 1 - c
        col = k if m in (JQ, AQ) else column(dd)
        dst = st.at[slot, m, pl.ds(pl.multiple_of(d * half, half), half)]
        remote = copy(src, dst, xs.at[m, dd, hf], xr.at[slot, m, d], (2 * col + hf, 2 * z + dd))
        local = pltpu.make_async_copy(src, dst, xr.at[slot, m, d])
        stays = jnp.logical_and(d == dd, c == hf)
        if m == CP:
            stays = jnp.logical_and(stays, c == dd)
        return local, remote, stays

    def scatter_all(m, act_local, act_remote, when=None):
        for dd in range(2):
            for hf in range(2):
                local, remote, stays = scatter(m, dd, hf)
                ok = True if when is None else (d == dd) == when
                if m == AP:

                    @pl.when(jnp.logical_and(ok, c != dd))
                    def _():
                        act_remote(remote)

                else:

                    @pl.when(jnp.logical_and(ok, stays))
                    def _():
                        act_local(local)

                    @pl.when(jnp.logical_and(ok, jnp.logical_not(stays)))
                    def _():
                        act_remote(remote)

    def begin(cp):
        cp.start()

    def sent(cp):
        cp.wait_send()

    def nothing(cp):
        pass

    def addend_c(dd, act_local, act_remote):
        src = ins[dd].at[C]
        dst = addc.at[pl.ds(pl.multiple_of(d * half, half), half)]
        to = (jnp.where(same, tm, flip), jnp.where(same, 2 * z + dd, 2 * zc + dd))
        remote = copy(src, dst, acs.at[dd], acr.at[d], to)
        stays = jnp.logical_and(same, d == dd)

        @pl.when(stays)
        def _():
            act_local(pltpu.make_async_copy(src, dst, acr.at[d]))

        @pl.when(jnp.logical_not(stays))
        def _():
            act_remote(remote)

    def addend_j(dd):
        dst = addj.at[0, pl.ds(pl.multiple_of(d * half, half), half)]
        return copy(ins[dd].at[J], dst, ajs.at[dd], ajr.at[d], (2 * column(dd) + 1 - c, 2 * z + dd))

    scatter_all(JQ, begin, begin, True)
    scatter_all(JQ, begin, begin, False)
    scatter_all(AQ, begin, begin, True)
    scatter_all(CP, begin, begin, True)
    scatter_all(CP, begin, begin, False)
    scatter_all(AQ, begin, begin, False)
    scatter_all(AP, begin, begin)
    for dd in range(2):
        addend_c(dd, begin, begin)
        addend_j(dd).start()

    mycols = pl.ds(pl.multiple_of(c * wide, wide), wide)
    sibcols = pl.ds(pl.multiple_of((1 - c) * wide, wide), wide)

    def staged(pair, m):
        if m == AP:
            return st.at[d, jnp.where(pair == d, AP, AQ)]
        return st.at[pair, m]

    def hrows(hh):
        return pl.ds(pl.multiple_of(hh * half, half), half)

    def zcopy(pair, m, hh):
        kind = jnp.where(pair == q, 0, 1)
        to = (tm, 2 * jnp.where(pair == q, zp, zc) + d)
        return copy(staged(pair, m).at[hrows(hh)], gat1.at[m, piece(z, hh), mycols], zs.at[pair, m, hh],
                    zr.at[kind, m, hh], to)

    def zsend(pair, m, hh, fresh=True):
        if fresh:
            arrived(st.at[pair, m, hrows(hh)], xs.at[m, 0, 0], xr.at[pair, m, hh])
        zcopy(pair, m, hh).start()

    def owncopy(m):
        src = staged(q, m)
        dst = gat1.at[m, block(z), mycols]
        return pltpu.make_async_copy(src, dst, las.at[m]), copy(src, dst, vs.at[3, m], vr.at[3, m], sibling)

    def start_own(m):
        for cp in owncopy(m):
            cp.start()

    def relay(m, hh):
        ref = gat1.at[m, piece(zc, hh), mycols]
        return copy(ref, ref, rs.at[m, hh], zr.at[2, m, hh], partner)

    def side(kind, m, b):
        ref = gat1.at[m, block(b), mycols]
        return copy(ref, ref, vs.at[kind, m], vr.at[kind, m], sibling)

    source = {0: zp, 1: zc, 2: last}

    def take(kind, m):
        for hh in range(2):
            arrived(gat1.at[m, piece(source[kind], hh), mycols], rs.at[m, hh], zr.at[kind, m, hh])
            if kind == 1:
                relay(m, hh).start()
        side(kind, m, source[kind]).start()

    def side_arrived(m, kinds=(3, 1, 0, 2)):
        if 3 in kinds:
            owncopy(m)[0].wait()
        for kind, b in ((3, z), (1, zc), (0, zp), (2, last)):
            if kind in kinds:
                arrived(gat1.at[m, block(b), sibcols], vs.at[kind, m], vr.at[kind, m])

    zsend(q, JQ, d)
    zsend(1 - q, JQ, d)
    zsend(1 - d, CP, d)
    zsend(q, AQ, d)
    zsend(1 - q, AQ, d)
    zsend(q, JQ, 1 - d)
    zsend(1 - q, JQ, 1 - d)
    start_own(JQ)
    take(1, JQ)
    zsend(d, CP, d)
    zsend(1 - d, CP, 1 - d)
    zsend(d, CP, 1 - d)
    start_own(CP)
    take(0, JQ)
    take(1, CP)
    zsend(q, AQ, 1 - d)
    zsend(1 - q, AQ, 1 - d)
    start_own(AQ)
    take(1, AQ)
    zsend(1 - d, AP, d, False)
    zsend(1 - d, AP, 1 - d, False)
    zsend(d, AP, d)
    zsend(d, AP, 1 - d)
    start_own(AP)
    take(0, CP)
    take(2, JQ)
    take(2, CP)

    def addend_on():
        return copy(addj.at[0], addj.at[1], afs.at[0], afr.at[0], (flip, 2 * zc + d))

    def dot(a, b):
        return jnp.dot(a, b, preferred_element_type=F32)

    tiles = [slice(i * rows, (i + 1) * rows) for i in range(4)]

    def fill_k(gat):
        @pl.loop(0, 4)
        def _(b):
            for t in tiles:
                kmat[block(b), t] = dot(gat[CP, block(b), :], gat[JQ, :, t]).astype(BF)

    def chain(s):
        for t in tiles:
            wl[s, t] = (wa[s, t].astype(F32) - dot(wa[s, :], kmat[:, t])).astype(BF)
        for t in tiles:
            wt[s, t] = dot(wl[s, :], kmat[:, t]).astype(BF)
        for t in tiles:
            wa[s, t] = (wl[s, t].astype(F32) + dot(wt[s, :], kmat[:, t])).astype(BF)

    top = slice(0, rows)
    low = slice(rows, 2 * rows)

    def middle(gat):
        for t in tiles:
            wg[:, t] = dot(wa[top, :], gat[CP, :, t]).astype(BF)

    def cov(gat, t, base):
        prod = lax.dot_general(wg[...], gat[AQ, t, :], (((1,), (1,)), ((), ())), preferred_element_type=F32)
        return (prod + base.astype(F32)).astype(BF)

    def info(gat):
        columns = gat[AP, :, block(r)]
        for t in tiles:
            wa[top, t] = lax.dot_general(columns, gat[JQ, :, t], (((0,), (0,)), ((), ())),
                                         preferred_element_type=F32).astype(BF)
        chain(top)

    side_arrived(JQ)
    side_arrived(CP)
    fill_k(gat1)
    side_arrived(AQ, (3, 1))
    wa[top, :] = gat1[AQ, block(r), :]
    chain(top)
    take(0, AQ)
    middle(gat1)
    take(1, AP)
    take(2, AQ)
    side_arrived(AQ, (0, 2))

    first = jnp.where(d == 0, segment >= 1, segment < 15)
    second = jnp.where(d == 0, segment >= 2, segment < 14)

    for hh in range(2):
        arrived(addc.at[hrows(hh)], acs.at[0], acr.at[hh])
    left = slice(0, wide)
    right = slice(wide, n)

    def cross2(i):
        src, dst = (
            (cov1.at[:, left], gat2.at[CP, block(r), left]),
            (cov1.at[:, right], gat2.at[CP, block(r), right]),
            (gat2.at[AQ, block(r), right], gat2.at[AP, block(r), right]),
            (gat2.at[AQ, block(r), left], gat2.at[AP, block(r), left]),
            (gat2.at[AQ, block(rp), left], gat2.at[AP, block(rp), left]),
            (gat2.at[JQ, block(r)], add2),
        )[i]
        return copy(src, dst, c2s.at[i], c2r.at[i], following)

    def cross_wait(i):
        dst = (
            gat2.at[CP, block(r), left],
            gat2.at[CP, block(r), right],
            gat2.at[AP, block(r), right],
            gat2.at[AP, block(r), left],
            gat2.at[AP, block(rp), left],
            add2,
        )[i]
        arrived(dst, c2s.at[i], c2r.at[i])

    pair_refs = (
        lambda b: gat2.at[JQ, block(b), left],
        lambda b: gat2.at[JQ, block(b), right],
        lambda b: gat2.at[CP, block(b), left],
        lambda b: gat2.at[CP, block(b), right],
        lambda b: gat2.at[AP, block(b), right],
    )

    def pair2(i):
        ref = pair_refs[i](r)
        return copy(ref, ref, p2s.at[i], p2r.at[i], partner)

    def pair_wait(i):
        arrived(pair_refs[i](rp), p2s.at[i], p2r.at[i])

    side_refs = (
        lambda a, b: gat2.at[JQ, block(a)],
        lambda a, b: gat2.at[JQ, block(b)],
        lambda a, b: gat2.at[CP, block(a)],
        lambda a, b: gat2.at[CP, block(b)],
        lambda a, b: gat2.at[AQ, block(a)],
        lambda a, b: gat2.at[AQ, block(b)],
        lambda a, b: gat2.at[AP, block(a), right],
        lambda a, b: gat2.at[AP, block(b), left],
        lambda a, b: gat2.at[AP, block(b), right],
        lambda a, b: gat2.at[AP, block(a), left],
    )

    def side2(i):
        ref = side_refs[i](r, rp)
        return copy(ref, ref, v2s.at[i], v2r.at[i], sibling)

    def side2_wait(*which):
        for i in which:
            arrived(side_refs[i](rq, rpq), v2s.at[i], v2r.at[i])

    for i in range(2):
        for t in tiles[2 * i : 2 * i + 2]:
            base = addc[:, t]
            cov1[:, t] = jnp.where(first, cov(gat1, t, base), base)
        cross2(i).start()
    for hh in range(2):
        arrived(addj.at[0, hrows(hh)], ajs.at[0], ajr.at[hh])

    @pl.when(aux)
    def _():
        addend_on().start()

    wa[low, :] = gat1[AQ, block(rp), :]
    chain(low)
    take(0, AP)
    take(2, AP)
    side_arrived(AP)

    def trans(s, b, ts):
        for t in ts:
            gat2[AQ, block(b), t] = jnp.where(first, dot(wa[s, :], gat1[AP, :, t]).astype(BF),
                                              gat1[AQ, block(b), t])

    trans(top, r, tiles[2:])
    cross2(2).start()
    trans(top, r, tiles[:2])
    cross2(3).start()
    trans(low, rp, tiles[:2])
    cross2(4).start()
    trans(low, rp, tiles[2:])
    side2(4).start()
    side2(5).start()
    cross_wait(0)
    pair2(2).start()

    info(gat1)
    mine = jnp.where(same, 0, 1)

    @pl.when(aux)
    def _():
        arrived(addj.at[1], afs.at[0], afr.at[0])

    for i in range(2):
        for t in tiles[2 * i : 2 * i + 2]:
            value = (dot(wa[top, :], gat1[AP, :, t]) + addj[mine, :, t].astype(F32)).astype(BF)
            gat2[JQ, block(r), t] = jnp.where(first, value, gat1[JQ, block(r), t])
        pair2(i).start()
    side2(0).start()
    cross2(5).start()
    cross_wait(1)
    pair2(3).start()
    side2(2).start()

    cross_wait(2)
    pair2(4).start()
    side2(6).start()
    for i in (2, 0, 1, 3):
        pair_wait(i)
    side2(3).start()
    side2(1).start()
    side2_wait(0, 1, 2, 3)
    fill_k(gat2)
    wa[top, :] = gat2[AQ, block(r), :]
    chain(top)
    middle(gat2)

    target = 2 * k + q

    def deliver(m, i, act_local, act_remote):
        cols = (left, right)[i]
        for hf in range(2):
            stays = jnp.logical_and(same, d == hf)
            src = res.at[m, pl.ds(hf * half, half), cols]
            dst = out.at[d, m, :, cols]

            @pl.when(stays)
            def _():
                act_local(pltpu.make_async_copy(src, dst, outs.at[hf, m, i]))

            @pl.when(jnp.logical_not(stays))
            def _():
                act_remote(copy(src, dst, outs.at[hf, m, i], outr.at[d, m, i], (target, 2 * r + hf)))

    def done(cp):
        cp.wait()

    def trans2(i):
        for t in tiles[2 * i : 2 * i + 2]:
            res[A, :, t] = jnp.where(second, dot(wa[top, :], gat2[AP, :, t]).astype(BF), gat2[AQ, block(r), t])
        deliver(A, i, begin, begin)

    side2_wait(4, 5)
    for i in range(2):
        for t in tiles[2 * i : 2 * i + 2]:
            base = cov1[:, t]
            res[C, :, t] = jnp.where(second, cov(gat2, t, base), base)
        deliver(C, i, begin, begin)
    cross_wait(3)
    side2(9).start()
    pair_wait(4)
    side2(8).start()
    side2_wait(6, 8)
    trans2(1)
    cross_wait(4)
    side2(7).start()
    side2_wait(7, 9)
    trans2(0)
    info(gat2)
    cross_wait(5)
    for i in range(2):
        for t in tiles[2 * i : 2 * i + 2]:
            value = (dot(wa[top, :], gat2[AP, :, t]) + add2[:, t].astype(F32)).astype(BF)
            res[J, :, t] = jnp.where(second, value, gat2[JQ, block(r), t])
        deliver(J, i, begin, begin)

    for m in (JQ, CP, AQ, AP):
        scatter_all(m, nothing, sent)
        owncopy(m)[1].wait_send()
        for hh in range(2):
            relay(m, hh).wait_send()
            for pair in range(2):
                zcopy(pair, m, hh).wait_send()
        for kind in range(3):
            side(kind, m, source[kind]).wait_send()
    for dd in range(2):
        addend_c(dd, nothing, sent)
        addend_j(dd).wait_send()

    @pl.when(aux)
    def _():
        addend_on().wait_send()

    for i in range(6):
        cross2(i).wait_send()
    for i in range(5):
        pair2(i).wait_send()
    for i in range(10):
        side2(i).wait_send()
    for m in range(3):
        for i, cols in enumerate((left, right)):
            deliver(m, i, done, sent)
            arrived(out.at[1 - d, m, :, cols], outs.at[0, m, i], outr.at[1 - d, m, i])

            @pl.when(aux)
            def _():
                arrived(out.at[d, m, :, cols], outs.at[0, m, i], outr.at[d, m, i])


def shards(forward_element, backward_element):
    fwd = forward_element[:, 0]
    bwd = backward_element[:, 0]
    _, half, n = fwd.shape
    rows = n // 4
    dma = pltpu.SemaphoreType.DMA
    anywhere = pl.BlockSpec(memory_space=pl.ANY)
    joint = pl.pallas_call(
        kernel,
        out_shape=jax.ShapeDtypeStruct((2, 3, half, n), BF),
        in_specs=[anywhere, anywhere],
        out_specs=anywhere,
        scratch_shapes=[
            pltpu.VMEM((2, 4, rows, n // 2), BF),
            pltpu.VMEM((4, n, n), BF),
            pltpu.VMEM((4, n, n), BF),
            pltpu.VMEM((n, n), BF),
            pltpu.VMEM((2 * rows, n), BF),
            pltpu.VMEM((2 * rows, n), BF),
            pltpu.VMEM((2 * rows, n), BF),
            pltpu.VMEM((rows, n), BF),
            pltpu.VMEM((rows, n), BF),
            pltpu.VMEM((3, rows, n), BF),
            pltpu.VMEM((rows, n), BF),
            pltpu.VMEM((2, rows, n), BF),
            pltpu.VMEM((rows, n), BF),
            dma((4, 2, 2)), dma((2, 4, 2)), dma((2, 4, 2)), dma((3, 4, 2)), dma((4, 2)), dma((4, 4)), dma((4, 4)),
            dma((4,)), dma((2,)), dma((2,)), dma((2,)), dma((2,)), dma((1,)), dma((1,)),
            dma((6,)), dma((6,)), dma((5,)), dma((5,)), dma((10,)), dma((10,)), dma((2, 3, 2)), dma((2, 3, 2)),
        ],
        compiler_params=pltpu.CompilerParams(
            has_side_effects=True, collective_id=0, vmem_limit_bytes=60000 * 1024
        ),
    )(fwd, bwd)
    return (joint[0][:, None], joint[1][:, None])


def solution(mesh):
    spec = P(None, "tm", "panel", None)
    return jax.shard_map(shards, mesh=mesh, in_specs=(spec, spec), out_specs=(spec, spec), check_vma=False)
```

```python
import jax
import jax.numpy as jnp
from jax import lax
from jax.experimental import pallas as pl
from jax.experimental.pallas import tpu as pltpu
from jax.sharding import PartitionSpec as P

MESH = pl.DeviceIdType.MESH
C, A, J = 0, 1, 2
JQ, CP, AQ, AP = 0, 1, 2, 3
BF = jnp.bfloat16
F32 = jnp.float32


def kernel(fwd, bwd, out, st, gat1, gat2, kmat, wa, wt, wl, wg, cov1, res, addc, addj, add2,
           xs, xr, zs, zr, rs, vs, vr, las, acs, acr, ajs, ajr, afs, afr,
           c2s, c2r, p2s, p2r, v2s, v2r, outs, outr):
    n = gat1.shape[-1]
    rows = n // 4
    half = rows // 2
    wide = n // 2
    tm = lax.axis_index("tm")
    p = lax.axis_index("panel")
    c = lax.rem(tm, 2)
    k = lax.div(tm, 2)
    z = lax.div(p, 2)
    d = lax.rem(p, 2)
    q = lax.div(z, 2)
    sgn = 1 - 2 * d
    same = c == q
    aux = jnp.logical_not(same)
    zc = 3 - z
    zp = z + 1 - 2 * lax.rem(z, 2)
    last = 3 - zp
    r = jnp.where(same, z, zc)
    rp = jnp.where(same, zp, last)
    rq = jnp.where(same, zc, z)
    rpq = jnp.where(same, last, zp)
    segment = 2 * k + q
    flip = tm + 1 - 2 * c
    partner = (tm, 2 * zp + d)
    across = (tm, 2 * zc + d)
    sibling = (flip, p)
    following = (lax.rem(tm + 2 * sgn + 16, 16), p)
    preceding = (lax.rem(tm - 2 * sgn + 16, 16), p)

    def copy(src, dst, ssem, rsem, dev):
        return pltpu.make_async_remote_copy(src, dst, ssem, rsem, device_id=dev, device_id_type=MESH)

    def block(i):
        return pl.ds(pl.multiple_of(i * rows, rows), rows)

    def piece(i, hh):
        return pl.ds(pl.multiple_of(i * rows + hh * half, half), half)

    def arrived(dst, ssem, rsem):
        copy(dst, dst, ssem, rsem, partner).wait_recv()

    barrier = pltpu.get_barrier_semaphore()

    def greet(dev):
        pl.semaphore_signal(barrier, inc=1, device_id=dev, device_id_type=MESH)

    before = lax.rem(k - sgn + 8, 8)
    greet(sibling)
    for core in range(2):
        greet((2 * k + core, 2 * z + 1 - d))
        greet((2 * before + 1 - d, 2 * z + core))
    greet(partner)
    greet(across)
    greet(preceding)

    @pl.when(aux)
    def _():
        for hh in range(2):
            greet((flip, 2 * zc + hh))

    pl.semaphore_wait(barrier, jnp.where(aux, 10, 8))

    ins = (fwd, bwd)
    mats = (J, C, A, A)

    def column(dd):
        return lax.rem(k + jnp.where(c == dd, 0, 1 - 2 * dd) + 8, 8)

    def scatter(m, dd, hf):
        src = ins[dd].at[mats[m], :, pl.ds(hf * wide, wide)]
        slot = c if m in (JQ, AQ) else 1 - c
        col = k if m in (JQ, AQ) else column(dd)
        dst = st.at[slot, m, pl.ds(pl.multiple_of(d * half, half), half)]
        remote = copy(src, dst, xs.at[m, dd, hf], xr.at[slot, m, d], (2 * col + hf, 2 * z + dd))
        local = pltpu.make_async_copy(src, dst, xr.at[slot, m, d])
        stays = jnp.logical_and(d == dd, c == hf)
        if m == CP:
            stays = jnp.logical_and(stays, c == dd)
        return local, remote, stays

    def scatter_all(m, act_local, act_remote, when=None):
        for dd in range(2):
            for hf in range(2):
                local, remote, stays = scatter(m, dd, hf)
                ok = True if when is None else (d == dd) == when
                if m == AP:

                    @pl.when(jnp.logical_and(ok, c != dd))
                    def _():
                        act_remote(remote)

                else:

                    @pl.when(jnp.logical_and(ok, stays))
                    def _():
                        act_local(local)

                    @pl.when(jnp.logical_and(ok, jnp.logical_not(stays)))
                    def _():
                        act_remote(remote)

    def begin(cp):
        cp.start()

    def sent(cp):
        cp.wait_send()

    def nothing(cp):
        pass

    def addend_c(dd, act_local, act_remote):
        src = ins[dd].at[C]
        dst = addc.at[pl.ds(pl.multiple_of(d * half, half), half)]
        to = (jnp.where(same, tm, flip), jnp.where(same, 2 * z + dd, 2 * zc + dd))
        remote = copy(src, dst, acs.at[dd], acr.at[d], to)
        stays = jnp.logical_and(same, d == dd)

        @pl.when(stays)
        def _():
            act_local(pltpu.make_async_copy(src, dst, acr.at[d]))

        @pl.when(jnp.logical_not(stays))
        def _():
            act_remote(remote)

    def addend_j(dd):
        dst = addj.at[0, pl.ds(pl.multiple_of(d * half, half), half)]
        return copy(ins[dd].at[J], dst, ajs.at[dd], ajr.at[d], (2 * column(dd) + 1 - c, 2 * z + dd))

    scatter_all(JQ, begin, begin, True)
    scatter_all(JQ, begin, begin, False)
    scatter_all(AQ, begin, begin, True)
    scatter_all(CP, begin, begin, True)
    scatter_all(CP, begin, begin, False)
    scatter_all(AQ, begin, begin, False)
    scatter_all(AP, begin, begin)
    for dd in range(2):
        addend_c(dd, begin, begin)
        addend_j(dd).start()

    mycols = pl.ds(pl.multiple_of(c * wide, wide), wide)
    sibcols = pl.ds(pl.multiple_of((1 - c) * wide, wide), wide)

    def staged(pair, m):
        if m == AP:
            return st.at[d, jnp.where(pair == d, AP, AQ)]
        return st.at[pair, m]

    def hrows(hh):
        return pl.ds(pl.multiple_of(hh * half, half), half)

    def zcopy(pair, m, hh):
        kind = jnp.where(pair == q, 0, 1)
        to = (tm, 2 * jnp.where(pair == q, zp, zc) + d)
        return copy(staged(pair, m).at[hrows(hh)], gat1.at[m, piece(z, hh), mycols], zs.at[pair, m, hh],
                    zr.at[kind, m, hh], to)

    def zsend(pair, m, hh, fresh=True):
        if fresh:
            arrived(st.at[pair, m, hrows(hh)], xs.at[m, 0, 0], xr.at[pair, m, hh])
        zcopy(pair, m, hh).start()

    def owncopy(m):
        src = staged(q, m)
        dst = gat1.at[m, block(z), mycols]
        return pltpu.make_async_copy(src, dst, las.at[m]), copy(src, dst, vs.at[3, m], vr.at[3, m], sibling)

    def start_own(m):
        for cp in owncopy(m):
            cp.start()

    def relay(m, hh):
        ref = gat1.at[m, piece(zc, hh), mycols]
        return copy(ref, ref, rs.at[m, hh], zr.at[2, m, hh], partner)

    def side(kind, m, b):
        ref = gat1.at[m, block(b), mycols]
        return copy(ref, ref, vs.at[kind, m], vr.at[kind, m], sibling)

    source = {0: zp, 1: zc, 2: last}

    def take(kind, m):
        for hh in range(2):
            arrived(gat1.at[m, piece(source[kind], hh), mycols], rs.at[m, hh], zr.at[kind, m, hh])
            if kind == 1:
                relay(m, hh).start()
        side(kind, m, source[kind]).start()

    def side_arrived(m, kinds=(3, 1, 0, 2)):
        if 3 in kinds:
            owncopy(m)[0].wait()
        for kind, b in ((3, z), (1, zc), (0, zp), (2, last)):
            if kind in kinds:
                arrived(gat1.at[m, block(b), sibcols], vs.at[kind, m], vr.at[kind, m])

    zsend(q, JQ, d)
    zsend(1 - q, JQ, d)
    zsend(1 - d, CP, d)
    zsend(q, AQ, d)
    zsend(1 - q, AQ, d)
    zsend(q, JQ, 1 - d)
    zsend(1 - q, JQ, 1 - d)
    start_own(JQ)
    take(1, JQ)
    zsend(d, CP, d)
    zsend(1 - d, CP, 1 - d)
    zsend(d, CP, 1 - d)
    start_own(CP)
    take(0, JQ)
    take(1, CP)
    zsend(q, AQ, 1 - d)
    zsend(1 - q, AQ, 1 - d)
    start_own(AQ)
    for hh in (d, 1 - d):
        arrived(st.at[d, AP, hrows(hh)], xs.at[AP, 0, 0], xr.at[d, AP, hh])
        zsend(1 - q, AP, hh, False)
    take(1, AQ)
    zsend(q, AP, d, False)
    zsend(q, AP, 1 - d, False)
    start_own(AP)
    take(0, CP)
    take(2, JQ)
    take(2, CP)

    def addend_on():
        return copy(addj.at[0], addj.at[1], afs.at[0], afr.at[0], (flip, 2 * zc + d))

    def dot(a, b):
        return jnp.dot(a, b, preferred_element_type=F32)

    tiles = [slice(i * rows, (i + 1) * rows) for i in range(4)]

    def fill_k(gat, one, two):
        @pl.loop(0, 2)
        def _(i):
            b = jnp.where(i == 0, one, two)
            for t in tiles:
                kmat[block(b), t] = dot(gat[CP, block(b), :], gat[JQ, :, t]).astype(BF)

    def chain(s):
        for t in tiles:
            wl[s, t] = (wa[s, t].astype(F32) - dot(wa[s, :], kmat[:, t])).astype(BF)
        for t in tiles:
            wt[s, t] = dot(wl[s, :], kmat[:, t]).astype(BF)
        for t in tiles:
            wa[s, t] = (wl[s, t].astype(F32) + dot(wt[s, :], kmat[:, t])).astype(BF)

    top = slice(0, rows)
    low = slice(rows, 2 * rows)

    def middle(gat):
        for t in tiles:
            wg[:, t] = dot(wa[top, :], gat[CP, :, t]).astype(BF)

    def cov(gat, t, base):
        prod = lax.dot_general(wg[...], gat[AQ, t, :], (((1,), (1,)), ((), ())), preferred_element_type=F32)
        return (prod + base.astype(F32)).astype(BF)

    def info(gat):
        columns = gat[AP, :, block(r)]
        for t in tiles:
            wa[top, t] = lax.dot_general(columns, gat[JQ, :, t], (((0,), (0,)), ((), ())),
                                         preferred_element_type=F32).astype(BF)
        chain(top)

    side_arrived(JQ)
    side_arrived(CP)
    fill_k(gat1, r, rq)
    fill_k(gat1, rp, rpq)
    side_arrived(AQ, (3, 1))
    wa[top, :] = gat1[AQ, block(r), :]
    chain(top)
    take(0, AQ)
    middle(gat1)
    take(1, AP)
    take(2, AQ)
    side_arrived(AQ, (0, 2))

    first = jnp.where(d == 0, segment >= 1, segment < 15)
    second = jnp.where(d == 0, segment >= 2, segment < 14)

    for hh in range(2):
        arrived(addc.at[hrows(hh)], acs.at[0], acr.at[hh])
    left = slice(0, wide)
    right = slice(wide, n)

    def cross2(i):
        src, dst = (
            (cov1.at[:, left], gat2.at[CP, block(r), left]),
            (cov1.at[:, right], gat2.at[CP, block(r), right]),
            (gat2.at[AQ, block(r), left], gat2.at[AP, block(r), left]),
            (gat2.at[AQ, block(r), right], gat2.at[AP, block(r), right]),
            (gat2.at[AQ, block(rp), left], gat2.at[AP, block(rp), left]),
            (gat2.at[JQ, block(r)], add2),
        )[i]
        return copy(src, dst, c2s.at[i], c2r.at[i], following)

    def cross_wait(i):
        dst = (
            gat2.at[CP, block(r), left],
            gat2.at[CP, block(r), right],
            gat2.at[AP, block(r), left],
            gat2.at[AP, block(r), right],
            gat2.at[AP, block(rp), left],
            add2,
        )[i]
        arrived(dst, c2s.at[i], c2r.at[i])

    pair_refs = (
        lambda b: gat2.at[JQ, block(b), left],
        lambda b: gat2.at[JQ, block(b), right],
        lambda b: gat2.at[CP, block(b), left],
        lambda b: gat2.at[CP, block(b), right],
        lambda b: gat2.at[AP, block(b), right],
    )

    def pair2(i):
        ref = pair_refs[i](r)
        return copy(ref, ref, p2s.at[i], p2r.at[i], partner)

    def pair_wait(i):
        arrived(pair_refs[i](rp), p2s.at[i], p2r.at[i])

    side_refs = (
        lambda a, b: gat2.at[JQ, block(a)],
        lambda a, b: gat2.at[JQ, block(b)],
        lambda a, b: gat2.at[CP, block(a)],
        lambda a, b: gat2.at[CP, block(b)],
        lambda a, b: gat2.at[AQ, block(a)],
        lambda a, b: gat2.at[AQ, block(b)],
        lambda a, b: gat2.at[AP, block(a), right],
        lambda a, b: gat2.at[AP, block(b), left],
        lambda a, b: gat2.at[AP, block(b), right],
        lambda a, b: gat2.at[AP, block(a), left],
    )

    def side2(i):
        ref = side_refs[i](r, rp)
        return copy(ref, ref, v2s.at[i], v2r.at[i], sibling)

    def side2_wait(*which):
        for i in which:
            arrived(side_refs[i](rq, rpq), v2s.at[i], v2r.at[i])

    for i in range(2):
        for t in tiles[2 * i : 2 * i + 2]:
            base = addc[:, t]
            cov1[:, t] = jnp.where(first, cov(gat1, t, base), base)
        cross2(i).start()
    for hh in range(2):
        arrived(addj.at[0, hrows(hh)], ajs.at[0], ajr.at[hh])

    @pl.when(aux)
    def _():
        addend_on().start()

    wa[low, :] = gat1[AQ, block(rp), :]
    chain(low)
    take(0, AP)
    take(2, AP)
    side_arrived(AP)

    def trans(s, b, ts):
        for t in ts:
            gat2[AQ, block(b), t] = jnp.where(first, dot(wa[s, :], gat1[AP, :, t]).astype(BF),
                                              gat1[AQ, block(b), t])

    trans(top, r, tiles[:2])
    cross2(2).start()
    trans(top, r, tiles[2:])
    cross2(3).start()
    trans(low, rp, tiles[:2])
    cross2(4).start()
    trans(low, rp, tiles[2:])
    side2(4).start()
    side2(5).start()
    cross_wait(0)
    pair2(2).start()

    info(gat1)
    mine = jnp.where(same, 0, 1)

    @pl.when(aux)
    def _():
        arrived(addj.at[1], afs.at[0], afr.at[0])

    for i in range(2):
        for t in tiles[2 * i : 2 * i + 2]:
            value = (dot(wa[top, :], gat1[AP, :, t]) + addj[mine, :, t].astype(F32)).astype(BF)
            gat2[JQ, block(r), t] = jnp.where(first, value, gat1[JQ, block(r), t])
        pair2(i).start()
    side2(0).start()
    cross2(5).start()
    cross_wait(1)
    pair2(3).start()
    side2(2).start()

    cross_wait(2)
    side2(9).start()
    for i in (2, 0, 1):
        pair_wait(i)
    side2(1).start()
    cross_wait(3)
    pair2(4).start()
    side2(6).start()
    side2_wait(0, 1, 2)
    fill_k(gat2, r, rq)
    pair_wait(3)
    side2(3).start()
    cross_wait(4)
    side2(7).start()
    side2_wait(3)
    fill_k(gat2, rp, rpq)
    wa[top, :] = gat2[AQ, block(r), :]
    chain(top)
    middle(gat2)

    target = 2 * k + q

    def deliver(m, i, act_local, act_remote):
        cols = (left, right)[i]
        for hf in range(2):
            stays = jnp.logical_and(same, d == hf)
            src = res.at[m, pl.ds(hf * half, half), cols]
            dst = out.at[d, m, :, cols]

            @pl.when(stays)
            def _():
                act_local(pltpu.make_async_copy(src, dst, outs.at[hf, m, i]))

            @pl.when(jnp.logical_not(stays))
            def _():
                act_remote(copy(src, dst, outs.at[hf, m, i], outr.at[d, m, i], (target, 2 * r + hf)))

    def done(cp):
        cp.wait()

    def trans2(i):
        for t in tiles[2 * i : 2 * i + 2]:
            res[A, :, t] = jnp.where(second, dot(wa[top, :], gat2[AP, :, t]).astype(BF), gat2[AQ, block(r), t])
        deliver(A, i, begin, begin)

    side2_wait(4, 5)
    for i in range(2):
        for t in tiles[2 * i : 2 * i + 2]:
            base = cov1[:, t]
            res[C, :, t] = jnp.where(second, cov(gat2, t, base), base)
        deliver(C, i, begin, begin)
    side2_wait(7, 9)
    trans2(0)
    pair_wait(4)
    side2(8).start()
    side2_wait(6, 8)
    trans2(1)
    info(gat2)
    cross_wait(5)
    for i in range(2):
        for t in tiles[2 * i : 2 * i + 2]:
            value = (dot(wa[top, :], gat2[AP, :, t]) + add2[:, t].astype(F32)).astype(BF)
            res[J, :, t] = jnp.where(second, value, gat2[JQ, block(r), t])
        deliver(J, i, begin, begin)

    for m in (JQ, CP, AQ, AP):
        scatter_all(m, nothing, sent)
        owncopy(m)[1].wait_send()
        for hh in range(2):
            relay(m, hh).wait_send()
            for pair in range(2):
                zcopy(pair, m, hh).wait_send()
        for kind in range(3):
            side(kind, m, source[kind]).wait_send()
    for dd in range(2):
        addend_c(dd, nothing, sent)
        addend_j(dd).wait_send()

    @pl.when(aux)
    def _():
        addend_on().wait_send()

    for i in range(6):
        cross2(i).wait_send()
    for i in range(5):
        pair2(i).wait_send()
    for i in range(10):
        side2(i).wait_send()
    for m in range(3):
        for i, cols in enumerate((left, right)):
            deliver(m, i, done, sent)
            arrived(out.at[1 - d, m, :, cols], outs.at[0, m, i], outr.at[1 - d, m, i])

            @pl.when(aux)
            def _():
                arrived(out.at[d, m, :, cols], outs.at[0, m, i], outr.at[d, m, i])


def shards(forward_element, backward_element):
    fwd = forward_element[:, 0]
    bwd = backward_element[:, 0]
    _, half, n = fwd.shape
    rows = n // 4
    dma = pltpu.SemaphoreType.DMA
    anywhere = pl.BlockSpec(memory_space=pl.ANY)
    joint = pl.pallas_call(
        kernel,
        out_shape=jax.ShapeDtypeStruct((2, 3, half, n), BF),
        in_specs=[anywhere, anywhere],
        out_specs=anywhere,
        scratch_shapes=[
            pltpu.VMEM((2, 4, rows, n // 2), BF),
            pltpu.VMEM((4, n, n), BF),
            pltpu.VMEM((4, n, n), BF),
            pltpu.VMEM((n, n), BF),
            pltpu.VMEM((2 * rows, n), BF),
            pltpu.VMEM((2 * rows, n), BF),
            pltpu.VMEM((2 * rows, n), BF),
            pltpu.VMEM((rows, n), BF),
            pltpu.VMEM((rows, n), BF),
            pltpu.VMEM((3, rows, n), BF),
            pltpu.VMEM((rows, n), BF),
            pltpu.VMEM((2, rows, n), BF),
            pltpu.VMEM((rows, n), BF),
            dma((4, 2, 2)), dma((2, 4, 2)), dma((2, 4, 2)), dma((3, 4, 2)), dma((4, 2)), dma((4, 4)), dma((4, 4)),
            dma((4,)), dma((2,)), dma((2,)), dma((2,)), dma((2,)), dma((1,)), dma((1,)),
            dma((6,)), dma((6,)), dma((5,)), dma((5,)), dma((10,)), dma((10,)), dma((2, 3, 2)), dma((2, 3, 2)),
        ],
        compiler_params=pltpu.CompilerParams(
            has_side_effects=True, collective_id=0, vmem_limit_bytes=60000 * 1024
        ),
    )(fwd, bwd)
    return (joint[0][:, None], joint[1][:, None])


def solution(mesh):
    spec = P(None, "tm", "panel", None)
    return jax.shard_map(shards, mesh=mesh, in_specs=(spec, spec), out_specs=(spec, spec), check_vma=False)
```

```python
import jax
import jax.numpy as jnp
from jax import lax
from jax.experimental import pallas as pl
from jax.experimental.pallas import tpu as pltpu
from jax.sharding import PartitionSpec as P

MESH = pl.DeviceIdType.MESH
C, A, J = 0, 1, 2
JQ, CP, AQ, AP = 0, 1, 2, 3
BF = jnp.bfloat16
F32 = jnp.float32


def kernel(fwd, bwd, out, st, gat1, gat2, kmat, wa, wt, wl, wg, cov1, res, addc, addj, add2,
           xs, xr, zs, zr, rs, vs, vr, las, acs, acr, ajs, ajr, afs, afr,
           c2s, c2r, p2s, p2r, v2s, v2r, outs, outr):
    n = gat1.shape[-1]
    rows = n // 4
    half = rows // 2
    wide = n // 2
    tm = lax.axis_index("tm")
    p = lax.axis_index("panel")
    c = lax.rem(tm, 2)
    k = lax.div(tm, 2)
    z = lax.div(p, 2)
    d = lax.rem(p, 2)
    q = lax.div(z, 2)
    sgn = 1 - 2 * d
    same = c == q
    aux = jnp.logical_not(same)
    zc = 3 - z
    zp = z + 1 - 2 * lax.rem(z, 2)
    last = 3 - zp
    r = jnp.where(same, z, zc)
    rp = jnp.where(same, zp, last)
    rq = jnp.where(same, zc, z)
    rpq = jnp.where(same, last, zp)
    segment = 2 * k + q
    flip = tm + 1 - 2 * c
    partner = (tm, 2 * zp + d)
    across = (tm, 2 * zc + d)
    sibling = (flip, p)
    following = (lax.rem(tm + 2 * sgn + 16, 16), p)
    preceding = (lax.rem(tm - 2 * sgn + 16, 16), p)

    def copy(src, dst, ssem, rsem, dev):
        return pltpu.make_async_remote_copy(src, dst, ssem, rsem, device_id=dev, device_id_type=MESH)

    def block(i):
        return pl.ds(pl.multiple_of(i * rows, rows), rows)

    def piece(i, hh):
        return pl.ds(pl.multiple_of(i * rows + hh * half, half), half)

    def arrived(dst, ssem, rsem):
        copy(dst, dst, ssem, rsem, partner).wait_recv()

    barrier = pltpu.get_barrier_semaphore()

    def greet(dev):
        pl.semaphore_signal(barrier, inc=1, device_id=dev, device_id_type=MESH)

    before = lax.rem(k - sgn + 8, 8)
    greet(sibling)
    for core in range(2):
        greet((2 * k + core, 2 * z + 1 - d))
        greet((2 * before + 1 - d, 2 * z + core))
    greet(partner)
    greet(across)
    greet(preceding)

    @pl.when(aux)
    def _():
        for hh in range(2):
            greet((flip, 2 * zc + hh))

    pl.semaphore_wait(barrier, jnp.where(aux, 10, 8))

    ins = (fwd, bwd)
    mats = (J, C, A, A)

    def column(dd):
        return lax.rem(k + jnp.where(c == dd, 0, 1 - 2 * dd) + 8, 8)

    def scatter(m, dd, hf):
        src = ins[dd].at[mats[m], :, pl.ds(hf * wide, wide)]
        slot = c if m in (JQ, AQ) else 1 - c
        col = k if m in (JQ, AQ) else column(dd)
        dst = st.at[slot, m, pl.ds(pl.multiple_of(d * half, half), half)]
        remote = copy(src, dst, xs.at[m, dd, hf], xr.at[slot, m, d], (2 * col + hf, 2 * z + dd))
        local = pltpu.make_async_copy(src, dst, xr.at[slot, m, d])
        stays = jnp.logical_and(d == dd, c == hf)
        if m == CP:
            stays = jnp.logical_and(stays, c == dd)
        return local, remote, stays

    def scatter_all(m, act_local, act_remote, when=None):
        for dd in range(2):
            for hf in range(2):
                local, remote, stays = scatter(m, dd, hf)
                ok = True if when is None else (d == dd) == when
                if m == AP:

                    @pl.when(jnp.logical_and(ok, c != dd))
                    def _():
                        act_remote(remote)

                else:

                    @pl.when(jnp.logical_and(ok, stays))
                    def _():
                        act_local(local)

                    @pl.when(jnp.logical_and(ok, jnp.logical_not(stays)))
                    def _():
                        act_remote(remote)

    def begin(cp):
        cp.start()

    def sent(cp):
        cp.wait_send()

    def nothing(cp):
        pass

    def addend_c(dd, act_local, act_remote):
        src = ins[dd].at[C]
        dst = addc.at[pl.ds(pl.multiple_of(d * half, half), half)]
        to = (jnp.where(same, tm, flip), jnp.where(same, 2 * z + dd, 2 * zc + dd))
        remote = copy(src, dst, acs.at[dd], acr.at[d], to)
        stays = jnp.logical_and(same, d == dd)

        @pl.when(stays)
        def _():
            act_local(pltpu.make_async_copy(src, dst, acr.at[d]))

        @pl.when(jnp.logical_not(stays))
        def _():
            act_remote(remote)

    def addend_j(dd):
        dst = addj.at[0, pl.ds(pl.multiple_of(d * half, half), half)]
        return copy(ins[dd].at[J], dst, ajs.at[dd], ajr.at[d], (2 * column(dd) + 1 - c, 2 * z + dd))

    scatter_all(JQ, begin, begin, True)
    scatter_all(JQ, begin, begin, False)
    scatter_all(AQ, begin, begin, True)
    scatter_all(CP, begin, begin, True)
    scatter_all(CP, begin, begin, False)
    scatter_all(AQ, begin, begin, False)
    scatter_all(AP, begin, begin)
    for dd in range(2):
        addend_c(dd, begin, begin)
        addend_j(dd).start()

    mycols = pl.ds(pl.multiple_of(c * wide, wide), wide)
    sibcols = pl.ds(pl.multiple_of((1 - c) * wide, wide), wide)

    def staged(pair, m):
        if m == AP:
            return st.at[d, jnp.where(pair == d, AP, AQ)]
        return st.at[pair, m]

    def hrows(hh):
        return pl.ds(pl.multiple_of(hh * half, half), half)

    def zcopy(pair, m, hh):
        kind = jnp.where(pair == q, 0, 1)
        to = (tm, 2 * jnp.where(pair == q, zp, zc) + d)
        return copy(staged(pair, m).at[hrows(hh)], gat1.at[m, piece(z, hh), mycols], zs.at[pair, m, hh],
                    zr.at[kind, m, hh], to)

    def zsend(pair, m, hh, fresh=True):
        if fresh:
            arrived(st.at[pair, m, hrows(hh)], xs.at[m, 0, 0], xr.at[pair, m, hh])
        zcopy(pair, m, hh).start()

    def owncopy(m):
        src = staged(q, m)
        dst = gat1.at[m, block(z), mycols]
        return pltpu.make_async_copy(src, dst, las.at[m]), copy(src, dst, vs.at[3, m], vr.at[3, m], sibling)

    def start_own(m):
        for cp in owncopy(m):
            cp.start()

    def relay(m, hh):
        ref = gat1.at[m, piece(zc, hh), mycols]
        return copy(ref, ref, rs.at[m, hh], zr.at[2, m, hh], partner)

    def side(kind, m, b):
        ref = gat1.at[m, block(b), mycols]
        return copy(ref, ref, vs.at[kind, m], vr.at[kind, m], sibling)

    source = {0: zp, 1: zc, 2: last}

    def take(kind, m):
        for hh in range(2):
            arrived(gat1.at[m, piece(source[kind], hh), mycols], rs.at[m, hh], zr.at[kind, m, hh])
            if kind == 1:
                relay(m, hh).start()
        side(kind, m, source[kind]).start()

    def side_arrived(m, kinds=(3, 1, 0, 2)):
        if 3 in kinds:
            owncopy(m)[0].wait()
        for kind, b in ((3, z), (1, zc), (0, zp), (2, last)):
            if kind in kinds:
                arrived(gat1.at[m, block(b), sibcols], vs.at[kind, m], vr.at[kind, m])

    zsend(q, JQ, d)
    zsend(1 - q, JQ, d)
    zsend(1 - d, CP, d)
    zsend(q, AQ, d)
    zsend(1 - q, AQ, d)
    zsend(q, JQ, 1 - d)
    zsend(1 - q, JQ, 1 - d)
    start_own(JQ)
    take(1, JQ)
    zsend(d, CP, d)
    zsend(1 - d, CP, 1 - d)
    zsend(d, CP, 1 - d)
    start_own(CP)
    take(0, JQ)
    take(1, CP)
    zsend(q, AQ, 1 - d)
    zsend(1 - q, AQ, 1 - d)
    start_own(AQ)
    for hh in (d, 1 - d):
        arrived(st.at[d, AP, hrows(hh)], xs.at[AP, 0, 0], xr.at[d, AP, hh])
        zsend(1 - q, AP, hh, False)
    take(1, AQ)
    zsend(q, AP, d, False)
    zsend(q, AP, 1 - d, False)
    start_own(AP)
    take(0, CP)
    take(2, JQ)
    take(2, CP)

    def addend_on():
        return copy(addj.at[0], addj.at[1], afs.at[0], afr.at[0], (flip, 2 * zc + d))

    def dot(a, b):
        return jnp.dot(a, b, preferred_element_type=F32)

    tiles = [slice(i * rows, (i + 1) * rows) for i in range(4)]

    def fill_k(gat, one, two):
        @pl.loop(0, 2)
        def _(i):
            b = jnp.where(i == 0, one, two)
            for t in tiles:
                kmat[block(b), t] = dot(gat[CP, block(b), :], gat[JQ, :, t]).astype(BF)

    def chain(s):
        for t in tiles:
            wl[s, t] = (wa[s, t].astype(F32) - dot(wa[s, :], kmat[:, t])).astype(BF)
        for t in tiles:
            wt[s, t] = dot(wl[s, :], kmat[:, t]).astype(BF)
        for t in tiles:
            wa[s, t] = (wl[s, t].astype(F32) + dot(wt[s, :], kmat[:, t])).astype(BF)

    top = slice(0, rows)
    low = slice(rows, 2 * rows)

    def middle(gat):
        for t in tiles:
            wg[:, t] = dot(wa[top, :], gat[CP, :, t]).astype(BF)

    def cov(gat, t, base):
        prod = lax.dot_general(wg[...], gat[AQ, t, :], (((1,), (1,)), ((), ())), preferred_element_type=F32)
        return (prod + base.astype(F32)).astype(BF)

    def info(gat):
        columns = gat[AP, :, block(r)]
        for t in tiles:
            wa[top, t] = lax.dot_general(columns, gat[JQ, :, t], (((0,), (0,)), ((), ())),
                                         preferred_element_type=F32).astype(BF)
        chain(top)

    side_arrived(JQ)
    side_arrived(CP)
    fill_k(gat1, r, rq)
    fill_k(gat1, rp, rpq)
    side_arrived(AQ, (3, 1))
    wa[top, :] = gat1[AQ, block(r), :]
    chain(top)
    take(0, AQ)
    middle(gat1)
    take(1, AP)
    take(2, AQ)
    side_arrived(AQ, (0, 2))

    first = jnp.where(d == 0, segment >= 1, segment < 15)
    second = jnp.where(d == 0, segment >= 2, segment < 14)

    for hh in range(2):
        arrived(addc.at[hrows(hh)], acs.at[0], acr.at[hh])
    left = slice(0, wide)
    right = slice(wide, n)

    def cross2(i):
        src, dst = (
            (cov1.at[:, left], gat2.at[CP, block(r), left]),
            (cov1.at[:, right], gat2.at[CP, block(r), right]),
            (gat2.at[AQ, block(r), left], gat2.at[AP, block(r), left]),
            (gat2.at[AQ, block(r), right], gat2.at[AP, block(r), right]),
            (gat2.at[AQ, block(rp), left], gat2.at[AP, block(rp), left]),
            (gat2.at[JQ, block(r)], add2),
        )[i]
        return copy(src, dst, c2s.at[i], c2r.at[i], following)

    def cross_wait(i):
        dst = (
            gat2.at[CP, block(r), left],
            gat2.at[CP, block(r), right],
            gat2.at[AP, block(r), left],
            gat2.at[AP, block(r), right],
            gat2.at[AP, block(rp), left],
            add2,
        )[i]
        arrived(dst, c2s.at[i], c2r.at[i])

    pair_refs = (
        lambda b: gat2.at[JQ, block(b), left],
        lambda b: gat2.at[JQ, block(b), right],
        lambda b: gat2.at[CP, block(b), left],
        lambda b: gat2.at[CP, block(b), right],
        lambda b: gat2.at[AP, block(b), right],
    )

    def pair2(i):
        ref = pair_refs[i](r)
        return copy(ref, ref, p2s.at[i], p2r.at[i], partner)

    def pair_wait(i):
        arrived(pair_refs[i](rp), p2s.at[i], p2r.at[i])

    side_refs = (
        lambda a, b: gat2.at[JQ, block(a)],
        lambda a, b: gat2.at[JQ, block(b)],
        lambda a, b: gat2.at[CP, block(a)],
        lambda a, b: gat2.at[CP, block(b)],
        lambda a, b: gat2.at[AQ, block(a)],
        lambda a, b: gat2.at[AQ, block(b)],
        lambda a, b: gat2.at[AP, block(a), right],
        lambda a, b: gat2.at[AP, block(b), left],
        lambda a, b: gat2.at[AP, block(b), right],
        lambda a, b: gat2.at[AP, block(a), left],
    )

    def side2(i):
        ref = side_refs[i](r, rp)
        return copy(ref, ref, v2s.at[i], v2r.at[i], sibling)

    def side2_wait(*which):
        for i in which:
            arrived(side_refs[i](rq, rpq), v2s.at[i], v2r.at[i])

    for i in range(2):
        for t in tiles[2 * i : 2 * i + 2]:
            base = addc[:, t]
            cov1[:, t] = jnp.where(first, cov(gat1, t, base), base)
        cross2(i).start()
    for hh in range(2):
        arrived(addj.at[0, hrows(hh)], ajs.at[0], ajr.at[hh])

    @pl.when(aux)
    def _():
        addend_on().start()

    wa[low, :] = gat1[AQ, block(rp), :]
    chain(low)
    take(0, AP)
    cross_wait(0)
    pair2(2).start()
    take(2, AP)
    side_arrived(AP)

    def trans(src, b, ts):
        for t in ts:
            gat2[AQ, block(b), t] = jnp.where(first, dot(src[...], gat1[AP, :, t]).astype(BF),
                                              gat1[AQ, block(b), t])

    trans(wa.at[top], r, tiles[:2])
    cross2(2).start()
    trans(wa.at[top], r, tiles[2:])
    cross2(3).start()
    side2(4).start()

    info(gat1)
    mine = jnp.where(same, 0, 1)

    @pl.when(aux)
    def _():
        arrived(addj.at[1], afs.at[0], afr.at[0])

    cross_wait(1)
    pair2(3).start()
    side2(2).start()
    for i in range(2):
        for t in tiles[2 * i : 2 * i + 2]:
            value = (dot(wa[top, :], gat1[AP, :, t]) + addj[mine, :, t].astype(F32)).astype(BF)
            gat2[JQ, block(r), t] = jnp.where(first, value, gat1[JQ, block(r), t])
        pair2(i).start()
    side2(0).start()
    trans(wa.at[low], rp, tiles[:2])
    cross2(4).start()
    cross2(5).start()
    trans(wa.at[low], rp, tiles[2:])
    side2(5).start()

    cross_wait(2)
    side2(9).start()
    for i in (2, 3, 0):
        pair_wait(i)
    side2(3).start()
    cross_wait(3)
    pair2(4).start()
    side2(6).start()
    pair_wait(1)
    side2(1).start()
    cross_wait(4)
    side2(7).start()
    side2_wait(0, 1, 2, 3)
    fill_k(gat2, r, rq)
    fill_k(gat2, rp, rpq)
    wa[top, :] = gat2[AQ, block(r), :]
    chain(top)
    middle(gat2)

    target = 2 * k + q

    def deliver(m, i, act_local, act_remote):
        cols = (left, right)[i]
        for hf in range(2):
            stays = jnp.logical_and(same, d == hf)
            src = res.at[m, pl.ds(hf * half, half), cols]
            dst = out.at[d, m, :, cols]

            @pl.when(stays)
            def _():
                act_local(pltpu.make_async_copy(src, dst, outs.at[hf, m, i]))

            @pl.when(jnp.logical_not(stays))
            def _():
                act_remote(copy(src, dst, outs.at[hf, m, i], outr.at[d, m, i], (target, 2 * r + hf)))

    def done(cp):
        cp.wait()

    def trans2(i):
        for t in tiles[2 * i : 2 * i + 2]:
            res[A, :, t] = jnp.where(second, dot(wa[top, :], gat2[AP, :, t]).astype(BF), gat2[AQ, block(r), t])
        deliver(A, i, begin, begin)

    side2_wait(4, 5)
    for i in range(2):
        for t in tiles[2 * i : 2 * i + 2]:
            base = cov1[:, t]
            res[C, :, t] = jnp.where(second, cov(gat2, t, base), base)
        deliver(C, i, begin, begin)
    side2_wait(7, 9)
    trans2(0)
    pair_wait(4)
    side2(8).start()
    side2_wait(6, 8)
    trans2(1)
    info(gat2)
    cross_wait(5)
    for i in range(2):
        for t in tiles[2 * i : 2 * i + 2]:
            value = (dot(wa[top, :], gat2[AP, :, t]) + add2[:, t].astype(F32)).astype(BF)
            res[J, :, t] = jnp.where(second, value, gat2[JQ, block(r), t])
        deliver(J, i, begin, begin)

    for m in (JQ, CP, AQ, AP):
        scatter_all(m, nothing, sent)
        owncopy(m)[1].wait_send()
        for hh in range(2):
            relay(m, hh).wait_send()
            for pair in range(2):
                zcopy(pair, m, hh).wait_send()
        for kind in range(3):
            side(kind, m, source[kind]).wait_send()
    for dd in range(2):
        addend_c(dd, nothing, sent)
        addend_j(dd).wait_send()

    @pl.when(aux)
    def _():
        addend_on().wait_send()

    for i in range(6):
        cross2(i).wait_send()
    for i in range(5):
        pair2(i).wait_send()
    for i in range(10):
        side2(i).wait_send()
    for m in range(3):
        for i, cols in enumerate((left, right)):
            deliver(m, i, done, sent)
            arrived(out.at[1 - d, m, :, cols], outs.at[0, m, i], outr.at[1 - d, m, i])

            @pl.when(aux)
            def _():
                arrived(out.at[d, m, :, cols], outs.at[0, m, i], outr.at[d, m, i])


def shards(forward_element, backward_element):
    fwd = forward_element[:, 0]
    bwd = backward_element[:, 0]
    _, half, n = fwd.shape
    rows = n // 4
    dma = pltpu.SemaphoreType.DMA
    anywhere = pl.BlockSpec(memory_space=pl.ANY)
    joint = pl.pallas_call(
        kernel,
        out_shape=jax.ShapeDtypeStruct((2, 3, half, n), BF),
        in_specs=[anywhere, anywhere],
        out_specs=anywhere,
        scratch_shapes=[
            pltpu.VMEM((2, 4, rows, n // 2), BF),
            pltpu.VMEM((4, n, n), BF),
            pltpu.VMEM((4, n, n), BF),
            pltpu.VMEM((n, n), BF),
            pltpu.VMEM((2 * rows, n), BF),
            pltpu.VMEM((2 * rows, n), BF),
            pltpu.VMEM((2 * rows, n), BF),
            pltpu.VMEM((rows, n), BF),
            pltpu.VMEM((rows, n), BF),
            pltpu.VMEM((3, rows, n), BF),
            pltpu.VMEM((rows, n), BF),
            pltpu.VMEM((2, rows, n), BF),
            pltpu.VMEM((rows, n), BF),
            dma((4, 2, 2)), dma((2, 4, 2)), dma((2, 4, 2)), dma((3, 4, 2)), dma((4, 2)), dma((4, 4)), dma((4, 4)),
            dma((4,)), dma((2,)), dma((2,)), dma((2,)), dma((2,)), dma((1,)), dma((1,)),
            dma((6,)), dma((6,)), dma((5,)), dma((5,)), dma((10,)), dma((10,)), dma((2, 3, 2)), dma((2, 3, 2)),
        ],
        compiler_params=pltpu.CompilerParams(
            has_side_effects=True, collective_id=0, vmem_limit_bytes=60000 * 1024
        ),
    )(fwd, bwd)
    return (joint[0][:, None], joint[1][:, None])


def solution(mesh):
    spec = P(None, "tm", "panel", None)
    return jax.shard_map(shards, mesh=mesh, in_specs=(spec, spec), out_specs=(spec, spec), check_vma=False)
```

```python
import jax
import jax.numpy as jnp
from jax import lax
from jax.experimental import pallas as pl
from jax.experimental.pallas import tpu as pltpu
from jax.sharding import PartitionSpec as P

MESH = pl.DeviceIdType.MESH
C, A, J = 0, 1, 2
JQ, CP, AQ, AP = 0, 1, 2, 3
BF = jnp.bfloat16
F32 = jnp.float32


def kernel(fwd, bwd, out, st, gat1, gat2, kmat, wa, wt, wl, wg, cov1, res, addc, addj, add2,
           xs, xr, zs, zr, rs, vs, vr, las, acs, acr, ajs, ajr, afs, afr,
           c2s, c2r, p2s, p2r, v2s, v2r, outs, outr):
    n = gat1.shape[-1]
    rows = n // 4
    half = rows // 2
    wide = n // 2
    tm = lax.axis_index("tm")
    p = lax.axis_index("panel")
    c = lax.rem(tm, 2)
    k = lax.div(tm, 2)
    z = lax.div(p, 2)
    d = lax.rem(p, 2)
    q = lax.div(z, 2)
    sgn = 1 - 2 * d
    same = c == q
    aux = jnp.logical_not(same)
    zc = 3 - z
    zp = z + 1 - 2 * lax.rem(z, 2)
    last = 3 - zp
    r = jnp.where(same, z, zc)
    rp = jnp.where(same, zp, last)
    rq = jnp.where(same, zc, z)
    rpq = jnp.where(same, last, zp)
    segment = 2 * k + q
    flip = tm + 1 - 2 * c
    partner = (tm, 2 * zp + d)
    across = (tm, 2 * zc + d)
    sibling = (flip, p)
    following = (lax.rem(tm + 2 * sgn + 16, 16), p)
    preceding = (lax.rem(tm - 2 * sgn + 16, 16), p)

    def copy(src, dst, ssem, rsem, dev):
        return pltpu.make_async_remote_copy(src, dst, ssem, rsem, device_id=dev, device_id_type=MESH)

    def block(i):
        return pl.ds(pl.multiple_of(i * rows, rows), rows)

    def piece(i, hh):
        return pl.ds(pl.multiple_of(i * rows + hh * half, half), half)

    def arrived(dst, ssem, rsem):
        copy(dst, dst, ssem, rsem, partner).wait_recv()

    barrier = pltpu.get_barrier_semaphore()

    def greet(dev):
        pl.semaphore_signal(barrier, inc=1, device_id=dev, device_id_type=MESH)

    before = lax.rem(k - sgn + 8, 8)
    greet(sibling)
    for core in range(2):
        greet((2 * k + core, 2 * z + 1 - d))
        greet((2 * before + 1 - d, 2 * z + core))
    greet(partner)
    greet(across)
    greet(preceding)

    @pl.when(aux)
    def _():
        for hh in range(2):
            greet((flip, 2 * zc + hh))

    pl.semaphore_wait(barrier, jnp.where(aux, 10, 8))

    ins = (fwd, bwd)
    mats = (J, C, A, A)

    def column(dd):
        return lax.rem(k + jnp.where(c == dd, 0, 1 - 2 * dd) + 8, 8)

    def scatter(m, dd, hf):
        src = ins[dd].at[mats[m], :, pl.ds(hf * wide, wide)]
        slot = c if m in (JQ, AQ) else 1 - c
        col = k if m in (JQ, AQ) else column(dd)
        dst = st.at[slot, m, pl.ds(pl.multiple_of(d * half, half), half)]
        remote = copy(src, dst, xs.at[m, dd, hf], xr.at[slot, m, d], (2 * col + hf, 2 * z + dd))
        local = pltpu.make_async_copy(src, dst, xr.at[slot, m, d])
        stays = jnp.logical_and(d == dd, c == hf)
        if m == CP:
            stays = jnp.logical_and(stays, c == dd)
        return local, remote, stays

    def scatter_all(m, act_local, act_remote, when=None):
        for dd in range(2):
            for hf in range(2):
                local, remote, stays = scatter(m, dd, hf)
                ok = True if when is None else (d == dd) == when
                if m == AP:

                    @pl.when(jnp.logical_and(ok, c != dd))
                    def _():
                        act_remote(remote)

                else:

                    @pl.when(jnp.logical_and(ok, stays))
                    def _():
                        act_local(local)

                    @pl.when(jnp.logical_and(ok, jnp.logical_not(stays)))
                    def _():
                        act_remote(remote)

    def begin(cp):
        cp.start()

    def sent(cp):
        cp.wait_send()

    def nothing(cp):
        pass

    def addend_c(dd, act_local, act_remote):
        src = ins[dd].at[C]
        dst = addc.at[pl.ds(pl.multiple_of(d * half, half), half)]
        to = (jnp.where(same, tm, flip), jnp.where(same, 2 * z + dd, 2 * zc + dd))
        remote = copy(src, dst, acs.at[dd], acr.at[d], to)
        stays = jnp.logical_and(same, d == dd)

        @pl.when(stays)
        def _():
            act_local(pltpu.make_async_copy(src, dst, acr.at[d]))

        @pl.when(jnp.logical_not(stays))
        def _():
            act_remote(remote)

    def addend_j(dd):
        dst = addj.at[0, pl.ds(pl.multiple_of(d * half, half), half)]
        return copy(ins[dd].at[J], dst, ajs.at[dd], ajr.at[d], (2 * column(dd) + 1 - c, 2 * z + dd))

    scatter_all(JQ, begin, begin, True)
    scatter_all(JQ, begin, begin, False)
    scatter_all(AQ, begin, begin, True)
    scatter_all(CP, begin, begin, True)
    scatter_all(CP, begin, begin, False)
    scatter_all(AQ, begin, begin, False)
    scatter_all(AP, begin, begin)
    for dd in range(2):
        addend_c(dd, begin, begin)
        addend_j(dd).start()

    mycols = pl.ds(pl.multiple_of(c * wide, wide), wide)
    sibcols = pl.ds(pl.multiple_of((1 - c) * wide, wide), wide)

    def staged(pair, m):
        if m == AP:
            return st.at[d, jnp.where(pair == d, AP, AQ)]
        return st.at[pair, m]

    def hrows(hh):
        return pl.ds(pl.multiple_of(hh * half, half), half)

    def zcopy(pair, m, hh):
        kind = jnp.where(pair == q, 0, 1)
        to = (tm, 2 * jnp.where(pair == q, zp, zc) + d)
        return copy(staged(pair, m).at[hrows(hh)], gat1.at[m, piece(z, hh), mycols], zs.at[pair, m, hh],
                    zr.at[kind, m, hh], to)

    def zsend(pair, m, hh, fresh=True):
        if fresh:
            arrived(st.at[pair, m, hrows(hh)], xs.at[m, 0, 0], xr.at[pair, m, hh])
        zcopy(pair, m, hh).start()

    def owncopy(m):
        src = staged(q, m)
        dst = gat1.at[m, block(z), mycols]
        return pltpu.make_async_copy(src, dst, las.at[m]), copy(src, dst, vs.at[3, m], vr.at[3, m], sibling)

    def start_own(m):
        for cp in owncopy(m):
            cp.start()

    def relay(m, hh):
        ref = gat1.at[m, piece(zc, hh), mycols]
        return copy(ref, ref, rs.at[m, hh], zr.at[2, m, hh], partner)

    def side(kind, m, b):
        ref = gat1.at[m, block(b), mycols]
        return copy(ref, ref, vs.at[kind, m], vr.at[kind, m], sibling)

    source = {0: zp, 1: zc, 2: last}

    def take(kind, m):
        for hh in range(2):
            arrived(gat1.at[m, piece(source[kind], hh), mycols], rs.at[m, hh], zr.at[kind, m, hh])
            if kind == 1:
                relay(m, hh).start()
        side(kind, m, source[kind]).start()

    def side_arrived(m, kinds=(3, 1, 0, 2)):
        if 3 in kinds:
            owncopy(m)[0].wait()
        for kind, b in ((3, z), (1, zc), (0, zp), (2, last)):
            if kind in kinds:
                arrived(gat1.at[m, block(b), sibcols], vs.at[kind, m], vr.at[kind, m])

    zsend(q, JQ, d)
    zsend(1 - q, JQ, d)
    zsend(1 - d, CP, d)
    zsend(q, AQ, d)
    zsend(1 - q, AQ, d)
    zsend(q, JQ, 1 - d)
    zsend(1 - q, JQ, 1 - d)
    start_own(JQ)
    take(1, JQ)
    zsend(d, CP, d)
    zsend(1 - d, CP, 1 - d)
    zsend(d, CP, 1 - d)
    start_own(CP)
    take(0, JQ)
    take(1, CP)
    zsend(q, AQ, 1 - d)
    zsend(1 - q, AQ, 1 - d)
    start_own(AQ)
    for hh in (d, 1 - d):
        arrived(st.at[d, AP, hrows(hh)], xs.at[AP, 0, 0], xr.at[d, AP, hh])
        zsend(1 - q, AP, hh, False)
    take(1, AQ)
    zsend(q, AP, d, False)
    zsend(q, AP, 1 - d, False)
    start_own(AP)
    take(0, CP)
    take(2, JQ)
    take(2, CP)

    def addend_on():
        return copy(addj.at[0], addj.at[1], afs.at[0], afr.at[0], (flip, 2 * zc + d))

    def dot(a, b):
        return jnp.dot(a, b, preferred_element_type=F32)

    tiles = [slice(i * rows, (i + 1) * rows) for i in range(4)]

    def fill_k(gat, ts):
        @pl.loop(0, 4)
        def _(b):
            for t in ts:
                kmat[block(b), t] = dot(gat[CP, block(b), :], gat[JQ, :, t]).astype(BF)

    def chain(s):
        for t in tiles:
            wl[s, t] = (wa[s, t].astype(F32) - dot(wa[s, :], kmat[:, t])).astype(BF)
        for t in tiles:
            wt[s, t] = dot(wl[s, :], kmat[:, t]).astype(BF)
        for t in tiles:
            wa[s, t] = (wl[s, t].astype(F32) + dot(wt[s, :], kmat[:, t])).astype(BF)

    top = slice(0, rows)
    low = slice(rows, 2 * rows)

    def middle(gat):
        for t in tiles:
            wg[:, t] = dot(wa[top, :], gat[CP, :, t]).astype(BF)

    def cov(gat, t, base):
        prod = lax.dot_general(wg[...], gat[AQ, t, :], (((1,), (1,)), ((), ())), preferred_element_type=F32)
        return (prod + base.astype(F32)).astype(BF)

    def info(gat):
        columns = gat[AP, :, block(r)]
        for t in tiles:
            wa[top, t] = lax.dot_general(columns, gat[JQ, :, t], (((0,), (0,)), ((), ())),
                                         preferred_element_type=F32).astype(BF)
        chain(top)

    side_arrived(JQ)
    side_arrived(CP)
    fill_k(gat1, tiles)
    side_arrived(AQ, (3, 1))
    wa[top, :] = gat1[AQ, block(r), :]
    chain(top)
    take(0, AQ)
    middle(gat1)
    take(1, AP)
    take(2, AQ)
    side_arrived(AQ, (0, 2))

    first = jnp.where(d == 0, segment >= 1, segment < 15)
    second = jnp.where(d == 0, segment >= 2, segment < 14)

    for hh in range(2):
        arrived(addc.at[hrows(hh)], acs.at[0], acr.at[hh])
    left = slice(0, wide)
    right = slice(wide, n)

    def cross2(i):
        src, dst = (
            (cov1.at[:, left], gat2.at[CP, block(r), left]),
            (cov1.at[:, right], gat2.at[CP, block(r), right]),
            (gat2.at[AQ, block(r), left], gat2.at[AP, block(r), left]),
            (gat2.at[AQ, block(r), right], gat2.at[AP, block(r), right]),
            (gat2.at[AQ, block(rp), tiles[0]], gat2.at[AP, block(rp), tiles[0]]),
            (gat2.at[JQ, block(r)], add2),
        )[i]
        return copy(src, dst, c2s.at[i], c2r.at[i], following)

    def cross_wait(i):
        dst = (
            gat2.at[CP, block(r), left],
            gat2.at[CP, block(r), right],
            gat2.at[AP, block(r), left],
            gat2.at[AP, block(r), right],
            gat2.at[AP, block(rp), tiles[0]],
            add2,
        )[i]
        arrived(dst, c2s.at[i], c2r.at[i])

    pair_refs = (
        lambda b: gat2.at[JQ, block(b), left],
        lambda b: gat2.at[JQ, block(b), right],
        lambda b: gat2.at[CP, block(b), left],
        lambda b: gat2.at[CP, block(b), right],
        lambda b: gat2.at[AP, block(b), right],
        lambda b: gat2.at[AP, block(b), tiles[1]],
    )

    def pair2(i):
        ref = pair_refs[i](r)
        return copy(ref, ref, p2s.at[i], p2r.at[i], partner)

    def pair_wait(i):
        arrived(pair_refs[i](rp), p2s.at[i], p2r.at[i])

    side_refs = (
        lambda a, b: gat2.at[JQ, block(a)],
        lambda a, b: gat2.at[JQ, block(b), left],
        lambda a, b: gat2.at[CP, block(a)],
        lambda a, b: gat2.at[CP, block(b)],
        lambda a, b: gat2.at[AQ, block(a)],
        lambda a, b: gat2.at[AQ, block(b)],
        lambda a, b: gat2.at[AP, block(a), right],
        lambda a, b: gat2.at[AP, block(b), left],
        lambda a, b: gat2.at[AP, block(b), right],
        lambda a, b: gat2.at[AP, block(a), left],
        lambda a, b: gat2.at[JQ, block(b), right],
    )

    def side2(i):
        ref = side_refs[i](r, rp)
        return copy(ref, ref, v2s.at[i], v2r.at[i], sibling)

    def side2_wait(*which):
        for i in which:
            arrived(side_refs[i](rq, rpq), v2s.at[i], v2r.at[i])

    for i in range(2):
        for t in tiles[2 * i : 2 * i + 2]:
            base = addc[:, t]
            cov1[:, t] = jnp.where(first, cov(gat1, t, base), base)
        cross2(i).start()
    for hh in range(2):
        arrived(addj.at[0, hrows(hh)], ajs.at[0], ajr.at[hh])

    @pl.when(aux)
    def _():
        addend_on().start()

    wa[low, :] = gat1[AQ, block(rp), :]
    chain(low)
    take(0, AP)
    cross_wait(0)
    pair2(2).start()
    take(2, AP)
    side_arrived(AP)

    def trans(src, b, ts):
        for t in ts:
            gat2[AQ, block(b), t] = jnp.where(first, dot(src[...], gat1[AP, :, t]).astype(BF),
                                              gat1[AQ, block(b), t])

    trans(wa.at[top], r, tiles[:2])
    cross2(2).start()
    trans(wa.at[top], r, tiles[2:])
    cross2(3).start()
    side2(4).start()

    info(gat1)
    mine = jnp.where(same, 0, 1)

    @pl.when(aux)
    def _():
        arrived(addj.at[1], afs.at[0], afr.at[0])

    cross_wait(1)
    pair2(3).start()
    side2(2).start()
    for i in range(2):
        for t in tiles[2 * i : 2 * i + 2]:
            value = (dot(wa[top, :], gat1[AP, :, t]) + addj[mine, :, t].astype(F32)).astype(BF)
            gat2[JQ, block(r), t] = jnp.where(first, value, gat1[JQ, block(r), t])
        pair2(i).start()
    side2(0).start()
    trans(wa.at[low], rp, tiles[:1])
    cross2(4).start()
    cross2(5).start()
    trans(wa.at[low], rp, tiles[1:])
    side2(5).start()

    cross_wait(2)
    pair2(5).start()
    side2(9).start()
    for i in (2, 3):
        pair_wait(i)
    side2(3).start()
    pair_wait(0)
    side2(1).start()
    cross_wait(3)
    pair2(4).start()
    side2(6).start()
    side2_wait(0, 1, 2, 3)
    fill_k(gat2, tiles[:2])
    pair_wait(1)
    side2(10).start()
    side2_wait(10)
    fill_k(gat2, tiles[2:])
    wa[top, :] = gat2[AQ, block(r), :]
    chain(top)
    cross_wait(4)
    pair_wait(5)
    side2(7).start()
    middle(gat2)

    target = 2 * k + q

    def deliver(m, i, act_local, act_remote):
        cols = (left, right)[i]
        for hf in range(2):
            stays = jnp.logical_and(same, d == hf)
            src = res.at[m, pl.ds(hf * half, half), cols]
            dst = out.at[d, m, :, cols]

            @pl.when(stays)
            def _():
                act_local(pltpu.make_async_copy(src, dst, outs.at[hf, m, i]))

            @pl.when(jnp.logical_not(stays))
            def _():
                act_remote(copy(src, dst, outs.at[hf, m, i], outr.at[d, m, i], (target, 2 * r + hf)))

    def done(cp):
        cp.wait()

    def trans2(i):
        for t in tiles[2 * i : 2 * i + 2]:
            res[A, :, t] = jnp.where(second, dot(wa[top, :], gat2[AP, :, t]).astype(BF), gat2[AQ, block(r), t])
        deliver(A, i, begin, begin)

    side2_wait(4, 5)
    for i in range(2):
        for t in tiles[2 * i : 2 * i + 2]:
            base = cov1[:, t]
            res[C, :, t] = jnp.where(second, cov(gat2, t, base), base)
        deliver(C, i, begin, begin)
    side2_wait(7, 9)
    trans2(0)
    pair_wait(4)
    side2(8).start()
    side2_wait(6, 8)
    trans2(1)
    info(gat2)
    cross_wait(5)
    for i in range(2):
        for t in tiles[2 * i : 2 * i + 2]:
            value = (dot(wa[top, :], gat2[AP, :, t]) + add2[:, t].astype(F32)).astype(BF)
            res[J, :, t] = jnp.where(second, value, gat2[JQ, block(r), t])
        deliver(J, i, begin, begin)

    for m in (JQ, CP, AQ, AP):
        scatter_all(m, nothing, sent)
        owncopy(m)[1].wait_send()
        for hh in range(2):
            relay(m, hh).wait_send()
            for pair in range(2):
                zcopy(pair, m, hh).wait_send()
        for kind in range(3):
            side(kind, m, source[kind]).wait_send()
    for dd in range(2):
        addend_c(dd, nothing, sent)
        addend_j(dd).wait_send()

    @pl.when(aux)
    def _():
        addend_on().wait_send()

    for i in range(6):
        cross2(i).wait_send()
    for i in range(6):
        pair2(i).wait_send()
    for i in range(11):
        side2(i).wait_send()
    for m in range(3):
        for i, cols in enumerate((left, right)):
            deliver(m, i, done, sent)
            arrived(out.at[1 - d, m, :, cols], outs.at[0, m, i], outr.at[1 - d, m, i])

            @pl.when(aux)
            def _():
                arrived(out.at[d, m, :, cols], outs.at[0, m, i], outr.at[d, m, i])


def shards(forward_element, backward_element):
    fwd = forward_element[:, 0]
    bwd = backward_element[:, 0]
    _, half, n = fwd.shape
    rows = n // 4
    dma = pltpu.SemaphoreType.DMA
    anywhere = pl.BlockSpec(memory_space=pl.ANY)
    joint = pl.pallas_call(
        kernel,
        out_shape=jax.ShapeDtypeStruct((2, 3, half, n), BF),
        in_specs=[anywhere, anywhere],
        out_specs=anywhere,
        scratch_shapes=[
            pltpu.VMEM((2, 4, rows, n // 2), BF),
            pltpu.VMEM((4, n, n), BF),
            pltpu.VMEM((4, n, n), BF),
            pltpu.VMEM((n, n), BF),
            pltpu.VMEM((2 * rows, n), BF),
            pltpu.VMEM((2 * rows, n), BF),
            pltpu.VMEM((2 * rows, n), BF),
            pltpu.VMEM((rows, n), BF),
            pltpu.VMEM((rows, n), BF),
            pltpu.VMEM((3, rows, n), BF),
            pltpu.VMEM((rows, n), BF),
            pltpu.VMEM((2, rows, n), BF),
            pltpu.VMEM((rows, n), BF),
            dma((4, 2, 2)), dma((2, 4, 2)), dma((2, 4, 2)), dma((3, 4, 2)), dma((4, 2)), dma((4, 4)), dma((4, 4)),
            dma((4,)), dma((2,)), dma((2,)), dma((2,)), dma((2,)), dma((1,)), dma((1,)),
            dma((6,)), dma((6,)), dma((6,)), dma((6,)), dma((11,)), dma((11,)), dma((2, 3, 2)), dma((2, 3, 2)),
        ],
        compiler_params=pltpu.CompilerParams(
            has_side_effects=True, collective_id=0, vmem_limit_bytes=60000 * 1024
        ),
    )(fwd, bwd)
    return (joint[0][:, None], joint[1][:, None])


def solution(mesh):
    spec = P(None, "tm", "panel", None)
    return jax.shard_map(shards, mesh=mesh, in_specs=(spec, spec), out_specs=(spec, spec), check_vma=False)
```

```python
import jax
import jax.numpy as jnp
from jax import lax
from jax.experimental import pallas as pl
from jax.experimental.pallas import tpu as pltpu
from jax.sharding import PartitionSpec as P

MESH = pl.DeviceIdType.MESH
C, A, J = 0, 1, 2
JQ, CP, AQ, AP = 0, 1, 2, 3
BF = jnp.bfloat16
F32 = jnp.float32


def kernel(fwd, bwd, out, st, gat1, gat2, kmat, wa, wt, wl, wg, cov1, res, addc, addj, add2,
           xs, xr, zs, zr, rs, vs, vr, las, acs, acr, ajs, ajr, afs, afr,
           c2s, c2r, p2s, p2r, v2s, v2r, outs, outr):
    n = gat1.shape[-1]
    rows = n // 4
    half = rows // 2
    wide = n // 2
    tm = lax.axis_index("tm")
    p = lax.axis_index("panel")
    c = lax.rem(tm, 2)
    k = lax.div(tm, 2)
    z = lax.div(p, 2)
    d = lax.rem(p, 2)
    q = lax.div(z, 2)
    sgn = 1 - 2 * d
    same = c == q
    aux = jnp.logical_not(same)
    zc = 3 - z
    zp = z + 1 - 2 * lax.rem(z, 2)
    last = 3 - zp
    r = jnp.where(same, z, zc)
    rp = jnp.where(same, zp, last)
    rq = jnp.where(same, zc, z)
    rpq = jnp.where(same, last, zp)
    segment = 2 * k + q
    flip = tm + 1 - 2 * c
    partner = (tm, 2 * zp + d)
    across = (tm, 2 * zc + d)
    sibling = (flip, p)
    following = (lax.rem(tm + 2 * sgn + 16, 16), p)
    preceding = (lax.rem(tm - 2 * sgn + 16, 16), p)

    def copy(src, dst, ssem, rsem, dev):
        return pltpu.make_async_remote_copy(src, dst, ssem, rsem, device_id=dev, device_id_type=MESH)

    def block(i):
        return pl.ds(pl.multiple_of(i * rows, rows), rows)

    def piece(i, hh):
        return pl.ds(pl.multiple_of(i * rows + hh * half, half), half)

    def arrived(dst, ssem, rsem):
        copy(dst, dst, ssem, rsem, partner).wait_recv()

    barrier = pltpu.get_barrier_semaphore()

    def greet(dev):
        pl.semaphore_signal(barrier, inc=1, device_id=dev, device_id_type=MESH)

    before = lax.rem(k - sgn + 8, 8)
    greet(sibling)
    for core in range(2):
        greet((2 * k + core, 2 * z + 1 - d))
        greet((2 * before + 1 - d, 2 * z + core))
    greet(partner)
    greet(across)
    greet(preceding)

    @pl.when(aux)
    def _():
        for hh in range(2):
            greet((flip, 2 * zc + hh))

    pl.semaphore_wait(barrier, jnp.where(aux, 10, 8))

    ins = (fwd, bwd)
    mats = (J, C, A, A)

    def column(dd):
        return lax.rem(k + jnp.where(c == dd, 0, 1 - 2 * dd) + 8, 8)

    def scatter(m, dd, hf):
        src = ins[dd].at[mats[m], :, pl.ds(hf * wide, wide)]
        slot = c if m in (JQ, AQ) else 1 - c
        col = k if m in (JQ, AQ) else column(dd)
        dst = st.at[slot, m, pl.ds(pl.multiple_of(d * half, half), half)]
        remote = copy(src, dst, xs.at[m, dd, hf], xr.at[slot, m, d], (2 * col + hf, 2 * z + dd))
        local = pltpu.make_async_copy(src, dst, xr.at[slot, m, d])
        stays = jnp.logical_and(d == dd, c == hf)
        if m == CP:
            stays = jnp.logical_and(stays, c == dd)
        return local, remote, stays

    def scatter_all(m, act_local, act_remote, when=None):
        for dd in range(2):
            for hf in range(2):
                local, remote, stays = scatter(m, dd, hf)
                ok = True if when is None else (d == dd) == when
                if m == AP:

                    @pl.when(jnp.logical_and(ok, c != dd))
                    def _():
                        act_remote(remote)

                else:

                    @pl.when(jnp.logical_and(ok, stays))
                    def _():
                        act_local(local)

                    @pl.when(jnp.logical_and(ok, jnp.logical_not(stays)))
                    def _():
                        act_remote(remote)

    def begin(cp):
        cp.start()

    def sent(cp):
        cp.wait_send()

    def nothing(cp):
        pass

    def addend_c(dd, act_local, act_remote):
        src = ins[dd].at[C]
        dst = addc.at[pl.ds(pl.multiple_of(d * half, half), half)]
        to = (jnp.where(same, tm, flip), jnp.where(same, 2 * z + dd, 2 * zc + dd))
        remote = copy(src, dst, acs.at[dd], acr.at[d], to)
        stays = jnp.logical_and(same, d == dd)

        @pl.when(stays)
        def _():
            act_local(pltpu.make_async_copy(src, dst, acr.at[d]))

        @pl.when(jnp.logical_not(stays))
        def _():
            act_remote(remote)

    def addend_j(dd):
        dst = addj.at[0, pl.ds(pl.multiple_of(d * half, half), half)]
        return copy(ins[dd].at[J], dst, ajs.at[dd], ajr.at[d], (2 * column(dd) + 1 - c, 2 * z + dd))

    scatter_all(JQ, begin, begin, True)
    scatter_all(JQ, begin, begin, False)
    scatter_all(AQ, begin, begin, True)
    scatter_all(CP, begin, begin, True)
    scatter_all(CP, begin, begin, False)
    scatter_all(AQ, begin, begin, False)
    scatter_all(AP, begin, begin)
    for dd in range(2):
        addend_c(dd, begin, begin)
        addend_j(dd).start()

    mycols = pl.ds(pl.multiple_of(c * wide, wide), wide)
    sibcols = pl.ds(pl.multiple_of((1 - c) * wide, wide), wide)

    def staged(pair, m):
        if m == AP:
            return st.at[d, jnp.where(pair == d, AP, AQ)]
        return st.at[pair, m]

    def hrows(hh):
        return pl.ds(pl.multiple_of(hh * half, half), half)

    def zcopy(pair, m, hh):
        kind = jnp.where(pair == q, 0, 1)
        to = (tm, 2 * jnp.where(pair == q, zp, zc) + d)
        return copy(staged(pair, m).at[hrows(hh)], gat1.at[m, piece(z, hh), mycols], zs.at[pair, m, hh],
                    zr.at[kind, m, hh], to)

    def zsend(pair, m, hh, fresh=True):
        if fresh:
            arrived(st.at[pair, m, hrows(hh)], xs.at[m, 0, 0], xr.at[pair, m, hh])
        zcopy(pair, m, hh).start()

    def owncopy(m):
        src = staged(q, m)
        dst = gat1.at[m, block(z), mycols]
        return pltpu.make_async_copy(src, dst, las.at[m]), copy(src, dst, vs.at[3, m], vr.at[3, m], sibling)

    def start_own(m):
        for cp in owncopy(m):
            cp.start()

    def relay(m, hh):
        ref = gat1.at[m, piece(zc, hh), mycols]
        return copy(ref, ref, rs.at[m, hh], zr.at[2, m, hh], partner)

    def side(kind, m, b):
        ref = gat1.at[m, block(b), mycols]
        return copy(ref, ref, vs.at[kind, m], vr.at[kind, m], sibling)

    source = {0: zp, 1: zc, 2: last}

    def take(kind, m):
        for hh in range(2):
            arrived(gat1.at[m, piece(source[kind], hh), mycols], rs.at[m, hh], zr.at[kind, m, hh])
            if kind == 1:
                relay(m, hh).start()
        side(kind, m, source[kind]).start()

    def side_arrived(m, kinds=(3, 1, 0, 2)):
        if 3 in kinds:
            owncopy(m)[0].wait()
        for kind, b in ((3, z), (1, zc), (0, zp), (2, last)):
            if kind in kinds:
                arrived(gat1.at[m, block(b), sibcols], vs.at[kind, m], vr.at[kind, m])

    zsend(q, JQ, d)
    zsend(1 - q, JQ, d)
    zsend(1 - d, CP, d)
    zsend(q, AQ, d)
    zsend(1 - q, AQ, d)
    zsend(q, JQ, 1 - d)
    zsend(1 - q, JQ, 1 - d)
    start_own(JQ)
    take(1, JQ)
    zsend(d, CP, d)
    zsend(1 - d, CP, 1 - d)
    zsend(d, CP, 1 - d)
    start_own(CP)
    take(0, JQ)
    take(1, CP)
    zsend(q, AQ, 1 - d)
    zsend(1 - q, AQ, 1 - d)
    start_own(AQ)
    for hh in (d, 1 - d):
        arrived(st.at[d, AP, hrows(hh)], xs.at[AP, 0, 0], xr.at[d, AP, hh])
        zsend(1 - q, AP, hh, False)
    take(1, AQ)
    zsend(q, AP, d, False)
    zsend(q, AP, 1 - d, False)
    start_own(AP)
    take(0, CP)
    take(2, JQ)
    take(2, CP)

    def addend_on():
        return copy(addj.at[0], addj.at[1], afs.at[0], afr.at[0], (flip, 2 * zc + d))

    def dot(a, b):
        return jnp.dot(a, b, preferred_element_type=F32)

    tiles = [slice(i * rows, (i + 1) * rows) for i in range(4)]

    def fill_k(gat, ts):
        @pl.loop(0, 4)
        def _(b):
            for t in ts:
                kmat[block(b), t] = dot(gat[CP, block(b), :], gat[JQ, :, t]).astype(BF)

    def chain(s):
        for t in tiles:
            wl[s, t] = (wa[s, t].astype(F32) - dot(wa[s, :], kmat[:, t])).astype(BF)
        for t in tiles:
            wt[s, t] = dot(wl[s, :], kmat[:, t]).astype(BF)
        for t in tiles:
            wa[s, t] = (wl[s, t].astype(F32) + dot(wt[s, :], kmat[:, t])).astype(BF)

    top = slice(0, rows)
    low = slice(rows, 2 * rows)

    def middle(gat, s):
        for t in tiles:
            wg[s, t] = dot(wa[s, :], gat[CP, :, t]).astype(BF)

    def cov(gat, s, t, base):
        prod = lax.dot_general(wg[s, :], gat[AQ, t, :], (((1,), (1,)), ((), ())), preferred_element_type=F32)
        return (prod + base.astype(F32)).astype(BF)

    def info(gat):
        columns = gat[AP, :, block(r)]
        for t in tiles:
            wa[top, t] = lax.dot_general(columns, gat[JQ, :, t], (((0,), (0,)), ((), ())),
                                         preferred_element_type=F32).astype(BF)
        chain(top)

    side_arrived(JQ)
    side_arrived(CP)
    fill_k(gat1, tiles)
    side_arrived(AQ, (3, 1))
    wa[top, :] = gat1[AQ, block(r), :]
    chain(top)
    take(0, AQ)
    middle(gat1, top)
    take(1, AP)
    take(2, AQ)
    side_arrived(AQ, (0, 2))

    first = jnp.where(d == 0, segment >= 1, segment < 15)
    second = jnp.where(d == 0, segment >= 2, segment < 14)

    for hh in range(2):
        arrived(addc.at[hrows(hh)], acs.at[0], acr.at[hh])
    left = slice(0, wide)
    right = slice(wide, n)

    def cross2(i):
        src, dst = (
            (cov1.at[:, left], gat2.at[CP, block(r), left]),
            (cov1.at[:, right], gat2.at[CP, block(r), right]),
            (gat2.at[AQ, block(r), left], gat2.at[AP, block(r), left]),
            (gat2.at[AQ, block(r), right], gat2.at[AP, block(r), right]),
            (gat2.at[AQ, block(rp), tiles[0]], gat2.at[AP, block(rp), tiles[0]]),
            (gat2.at[JQ, block(r)], add2),
        )[i]
        return copy(src, dst, c2s.at[i], c2r.at[i], following)

    def cross_wait(i):
        dst = (
            gat2.at[CP, block(r), left],
            gat2.at[CP, block(r), right],
            gat2.at[AP, block(r), left],
            gat2.at[AP, block(r), right],
            gat2.at[AP, block(rp), tiles[0]],
            add2,
        )[i]
        arrived(dst, c2s.at[i], c2r.at[i])

    pair_refs = (
        lambda b: gat2.at[JQ, block(b), left],
        lambda b: gat2.at[JQ, block(b), right],
        lambda b: gat2.at[CP, block(b), left],
        lambda b: gat2.at[CP, block(b), right],
        lambda b: gat2.at[AP, block(b), right],
        lambda b: gat2.at[AP, block(b), tiles[1]],
    )

    def pair2(i):
        ref = pair_refs[i](r)
        return copy(ref, ref, p2s.at[i], p2r.at[i], partner)

    def pair_wait(i):
        arrived(pair_refs[i](rp), p2s.at[i], p2r.at[i])

    side_refs = (
        lambda a, b: gat2.at[JQ, block(a)],
        lambda a, b: gat2.at[JQ, block(b), left],
        lambda a, b: gat2.at[CP, block(a)],
        lambda a, b: gat2.at[CP, block(b)],
        lambda a, b: gat2.at[AQ, block(a)],
        lambda a, b: gat2.at[AQ, block(b)],
        lambda a, b: gat2.at[AP, block(a), right],
        lambda a, b: gat2.at[AP, block(b), left],
        lambda a, b: gat2.at[AP, block(b), right],
        lambda a, b: gat2.at[AP, block(a), left],
        lambda a, b: gat2.at[JQ, block(b), right],
    )

    def side2(i):
        ref = side_refs[i](r, rp)
        return copy(ref, ref, v2s.at[i], v2r.at[i], sibling)

    def side2_wait(*which):
        for i in which:
            arrived(side_refs[i](rq, rpq), v2s.at[i], v2r.at[i])

    for i in range(2):
        for t in tiles[2 * i : 2 * i + 2]:
            base = addc[:, t]
            cov1[:, t] = jnp.where(first, cov(gat1, top, t, base), base)
        cross2(i).start()
    for hh in range(2):
        arrived(addj.at[0, hrows(hh)], ajs.at[0], ajr.at[hh])

    @pl.when(aux)
    def _():
        addend_on().start()

    wa[low, :] = gat1[AQ, block(rp), :]
    chain(low)
    take(0, AP)
    cross_wait(0)
    pair2(2).start()
    take(2, AP)
    side_arrived(AP)

    def trans(src, b, ts):
        for t in ts:
            gat2[AQ, block(b), t] = jnp.where(first, dot(src[...], gat1[AP, :, t]).astype(BF),
                                              gat1[AQ, block(b), t])

    trans(wa.at[top], r, tiles[:2])
    cross2(2).start()
    trans(wa.at[top], r, tiles[2:])
    cross2(3).start()
    side2(4).start()

    info(gat1)
    mine = jnp.where(same, 0, 1)

    @pl.when(aux)
    def _():
        arrived(addj.at[1], afs.at[0], afr.at[0])

    cross_wait(1)
    pair2(3).start()
    side2(2).start()
    for i in range(2):
        for t in tiles[2 * i : 2 * i + 2]:
            value = (dot(wa[top, :], gat1[AP, :, t]) + addj[mine, :, t].astype(F32)).astype(BF)
            gat2[JQ, block(r), t] = jnp.where(first, value, gat1[JQ, block(r), t])
        pair2(i).start()
    side2(0).start()
    trans(wa.at[low], rp, tiles[:1])
    cross2(4).start()
    cross2(5).start()
    trans(wa.at[low], rp, tiles[1:])
    side2(5).start()

    cross_wait(2)
    pair2(5).start()
    side2(9).start()
    for i in (2, 3):
        pair_wait(i)
    side2(3).start()
    pair_wait(0)
    side2(1).start()
    cross_wait(3)
    pair2(4).start()
    side2(6).start()
    side2_wait(0, 1, 2, 3)
    fill_k(gat2, tiles[:2])
    pair_wait(1)
    side2(10).start()
    side2_wait(10)
    fill_k(gat2, tiles[2:])
    wa[top, :] = gat2[AQ, block(r), :]
    far = hrows(1 - d)
    near = hrows(d)
    chain(far)
    middle(gat2, far)

    target = 2 * k + q

    def deliver(m, i, part, act_local, act_remote):
        cols = (left, right)[i]
        src = res.at[m, (far, near)[part], cols]
        dst = out.at[d, m, :, cols]
        hf = (1 - d, d)[part]
        remote = copy(src, dst, outs.at[part, m, i], outr.at[d, m, i], (target, 2 * r + hf))
        if part == 0:
            act_remote(remote)
            return

        @pl.when(same)
        def _():
            act_local(pltpu.make_async_copy(src, dst, outs.at[1, m, i]))

        @pl.when(aux)
        def _():
            act_remote(remote)

    def done(cp):
        cp.wait()

    def trans2(i):
        for t in tiles[2 * i : 2 * i + 2]:
            res[A, :, t] = jnp.where(second, dot(wa[top, :], gat2[AP, :, t]).astype(BF), gat2[AQ, block(r), t])
        for part in range(2):
            deliver(A, i, part, begin, begin)

    side2_wait(4, 5)
    for part, s in enumerate((far, near)):
        if part == 1:
            cross_wait(4)
            pair_wait(5)
            side2(7).start()
            chain(near)
            middle(gat2, near)
        for i in range(2):
            for t in tiles[2 * i : 2 * i + 2]:
                base = cov1[s, t]
                res[C, s, t] = jnp.where(second, cov(gat2, s, t, base), base)
            deliver(C, i, part, begin, begin)
    side2_wait(7, 9)
    trans2(0)
    pair_wait(4)
    side2(8).start()
    side2_wait(6, 8)
    trans2(1)
    info(gat2)
    cross_wait(5)
    for i in range(2):
        for t in tiles[2 * i : 2 * i + 2]:
            value = (dot(wa[top, :], gat2[AP, :, t]) + add2[:, t].astype(F32)).astype(BF)
            res[J, :, t] = jnp.where(second, value, gat2[JQ, block(r), t])
        for part in range(2):
            deliver(J, i, part, begin, begin)

    for m in (JQ, CP, AQ, AP):
        scatter_all(m, nothing, sent)
        owncopy(m)[1].wait_send()
        for hh in range(2):
            relay(m, hh).wait_send()
            for pair in range(2):
                zcopy(pair, m, hh).wait_send()
        for kind in range(3):
            side(kind, m, source[kind]).wait_send()
    for dd in range(2):
        addend_c(dd, nothing, sent)
        addend_j(dd).wait_send()

    @pl.when(aux)
    def _():
        addend_on().wait_send()

    for i in range(6):
        cross2(i).wait_send()
    for i in range(6):
        pair2(i).wait_send()
    for i in range(11):
        side2(i).wait_send()
    for m in range(3):
        for i, cols in enumerate((left, right)):
            for part in range(2):
                deliver(m, i, part, done, sent)
            arrived(out.at[1 - d, m, :, cols], outs.at[0, m, i], outr.at[1 - d, m, i])

            @pl.when(aux)
            def _():
                arrived(out.at[d, m, :, cols], outs.at[0, m, i], outr.at[d, m, i])


def shards(forward_element, backward_element):
    fwd = forward_element[:, 0]
    bwd = backward_element[:, 0]
    _, half, n = fwd.shape
    rows = n // 4
    dma = pltpu.SemaphoreType.DMA
    anywhere = pl.BlockSpec(memory_space=pl.ANY)
    joint = pl.pallas_call(
        kernel,
        out_shape=jax.ShapeDtypeStruct((2, 3, half, n), BF),
        in_specs=[anywhere, anywhere],
        out_specs=anywhere,
        scratch_shapes=[
            pltpu.VMEM((2, 4, rows, n // 2), BF),
            pltpu.VMEM((4, n, n), BF),
            pltpu.VMEM((4, n, n), BF),
            pltpu.VMEM((n, n), BF),
            pltpu.VMEM((2 * rows, n), BF),
            pltpu.VMEM((2 * rows, n), BF),
            pltpu.VMEM((2 * rows, n), BF),
            pltpu.VMEM((rows, n), BF),
            pltpu.VMEM((rows, n), BF),
            pltpu.VMEM((3, rows, n), BF),
            pltpu.VMEM((rows, n), BF),
            pltpu.VMEM((2, rows, n), BF),
            pltpu.VMEM((rows, n), BF),
            dma((4, 2, 2)), dma((2, 4, 2)), dma((2, 4, 2)), dma((3, 4, 2)), dma((4, 2)), dma((4, 4)), dma((4, 4)),
            dma((4,)), dma((2,)), dma((2,)), dma((2,)), dma((2,)), dma((1,)), dma((1,)),
            dma((6,)), dma((6,)), dma((6,)), dma((6,)), dma((11,)), dma((11,)), dma((2, 3, 2)), dma((2, 3, 2)),
        ],
        compiler_params=pltpu.CompilerParams(
            has_side_effects=True, collective_id=0, vmem_limit_bytes=60000 * 1024
        ),
    )(fwd, bwd)
    return (joint[0][:, None], joint[1][:, None])


def solution(mesh):
    spec = P(None, "tm", "panel", None)
    return jax.shard_map(shards, mesh=mesh, in_specs=(spec, spec), out_specs=(spec, spec), check_vma=False)
```
